512 devices in a mesh: theta: 64 (over z, y_hi, core), gz: 8 (over x, y_lo).
Axes of the slice: x: 4, y: 4 (y_hi: 2, y_lo: 2; y = y_hi * 2 + y_lo), z: 16, core: 2. Of those that a mesh axis runs over, the one named last changes fastest.
Arguments:
- fluid_state: float32 [8, 64, 1024, 128], P(None, 'gz', 'theta'), may hold values from -5 to 20, as said below
- levels: int32 [4, 128], P(None, 'theta'), may hold values from 0 to 1, as said below
- fine_rim: float32 [512, 2, 8, 1024], P('theta', None, None, 'gz'), may hold values from -1.5 to 3, as said below
- slot_owner: int32 [512], replicated, may hold values from 0 to 63, as said below
- slot_block: int32 [512], replicated, may hold values from 0 to 1
- slot_count: int32 [64], replicated, may hold values from 0 to 8, as said below
Outputs:
- residual: float32 [8, 64, 1024, 128], P(None, 'gz', 'theta')
- flux_mismatch: float32 [8, 64, 1024], P(None, 'gz', 'theta')
- inner_flux: float32 [8, 64, 1024], P(None, 'gz', 'theta')
The draws below stay inside these ranges and needn't reach their ends.
Inputs may be any that keep to these rules, and one draw needn't show every extreme that they name: `fluid_state`: density and pressure are positive; velocities and fields up to 1.5 in magnitude. `fine_rim`: primitive variables: density and pressure positive, velocity and field components up to 1.5 in magnitude. `levels`: each column is 1 on its first r blocks and 0 after, with at least one 1 and one 0. `slot_owner`: slot d * 8 + s belongs to theta device d; the valid slots of a device are its first slot_count[d]; values of other slots are arbitrary; every pair of owner and block is named by exactly two valid slots. `slot_count`: some device fills all 8 slots in every draw.
All inputs are finite; a program needn't handle non-finite values.
Results may differ from the reference program's by a relative error of at most 0.0003.
Values sent between devices are 32-bit elements; how exact they have to be, the bound alone decides.
A program may use at most 64 MiB of HBM per device.

```python
import math
import jax
import jax.numpy as jnp
from jax import lax

NR = 128
CT = 16
CZ = 8
FIELDS = 8
BT = 8
BR = 32
THETA_DEVS = 64
NT = 1024
NZ = 64
NRB = 4
NTB = 128
SLOTS = 8
SLOT_ALL = 512


GAMMA = 5.0 / 3.0


def primitive_draw(key, shape):
    keys = jax.random.split(key, 4)
    density = jnp.exp(jax.random.uniform(keys[0], shape, jnp.float32, math.log(0.5), math.log(2.0)))
    pressure = jnp.exp(jax.random.uniform(keys[1], shape, jnp.float32, math.log(0.2), math.log(2.0)))
    velocity = jnp.clip(0.5 * jax.random.normal(keys[2], (3,) + shape, jnp.float32), -1.5, 1.5)
    field = jnp.clip(0.6 * jax.random.normal(keys[3], (3,) + shape, jnp.float32), -1.5, 1.5)
    return (density, pressure, velocity, field)


def draw_fluid_state(key, part):
    density, pressure, velocity, field = primitive_draw(jax.random.fold_in(key, 11), (NZ, NT, NR))
    energy = pressure / (GAMMA - 1.0) + 0.5 * density * jnp.sum(velocity * velocity, axis=0) + 0.5 * jnp.sum(field * field, axis=0)
    return jnp.stack([density, density * velocity[0], density * velocity[1], density * velocity[2], energy, field[0], field[1], field[2]])


def draw_fine_rim(key, part):
    density, pressure, velocity, field = primitive_draw(jax.random.fold_in(key, 13), (SLOT_ALL, 2, NZ * 2 * BT))
    return jnp.stack([density, velocity[0], velocity[1], velocity[2], pressure, field[0], field[1], field[2]], axis=2)


def draw_levels(key, part):
    depth = jax.random.randint(jax.random.fold_in(key, 31), (NTB,), 1, NRB)
    return (jnp.arange(NRB)[:, None] < depth[None, :]).astype(jnp.int32)


def slot_tables(key):
    keys = jax.random.split(jax.random.fold_in(key, 23), 5)
    devices = THETA_DEVS
    mean_load = 2 * (CT // BT)
    pairs = devices // 2
    spread = jax.random.randint(keys[0], (pairs,), 0, mean_load + 1)
    forced = jax.random.randint(keys[1], (), 0, pairs)
    spread = jnp.where(jnp.arange(pairs) == forced, mean_load, spread)
    flips = jax.random.randint(keys[2], (pairs,), 0, 2)
    first_load = mean_load + spread * (1 - 2 * flips)
    loads = jnp.stack([first_load, 2 * mean_load - first_load], axis=1).reshape(devices)
    offsets = jnp.cumsum(loads) - loads
    total_targets = devices * mean_load
    order = jax.random.permutation(keys[3], total_targets)
    slot_pos = jnp.arange(SLOTS)
    wanted = offsets[:, None] + slot_pos[None, :]
    filler = jax.random.randint(keys[4], (devices, SLOTS), 0, total_targets)
    live_slots = slot_pos[None, :] < loads[:, None]
    picked = jnp.where(live_slots, wanted, filler)
    target = order[picked]
    owners = (target // mean_load).reshape(-1).astype(jnp.int32)
    block_ids = (target % mean_load // 2).reshape(-1).astype(jnp.int32)
    return (owners, block_ids, loads.astype(jnp.int32))


def draw_slot_owner(key, part):
    return slot_tables(key)[0]


def draw_slot_block(key, part):
    return slot_tables(key)[1]


def draw_slot_count(key, part):
    return slot_tables(key)[2]


def steps_of(stream_key, dims, pieces, smallest, largest):
    def one(dim, blocks):
        draws = jax.random.uniform(jax.random.fold_in(jax.random.fold_in(stream_key, 6), dim), (blocks,), jnp.float32, smallest / len(pieces), largest / len(pieces))
        return jnp.repeat(jnp.exp(draws), dims[dim] // blocks).reshape((-1,) + (1,) * (len(dims) - dim - 1))

    factor_of = one(*pieces[0])
    for cut in pieces[1:]:
        factor_of = factor_of * one(*cut)
    return factor_of


def setup_inputs(seed: int = 0) -> dict:
    arg_keys = jax.random.split(jax.random.key(seed), 7)
    return {
        "fluid_state": draw_fluid_state(jax.random.fold_in(arg_keys[6], 71), 0),
        "levels": draw_levels(jax.random.fold_in(arg_keys[6], 71), 0),
        "fine_rim": draw_fine_rim(jax.random.fold_in(arg_keys[6], 71), 0),
        "slot_owner": draw_slot_owner(jax.random.fold_in(arg_keys[6], 71), 0),
        "slot_block": draw_slot_block(jax.random.fold_in(arg_keys[6], 71), 0),
        "slot_count": draw_slot_count(jax.random.fold_in(arg_keys[6], 71), 0),
    }


GAMMA = 5.0 / 3.0
AXIS_FLIP = (1.0, -1.0, -1.0, 1.0, 1.0, -1.0, -1.0, 1.0)

def primitive(conserved):
    density = conserved[0]
    vel_r = conserved[1] / density
    vel_t = conserved[2] / density
    vel_z = conserved[3] / density
    kinetic = 0.5 * density * (vel_r * vel_r + vel_t * vel_t + vel_z * vel_z)
    magnetic = 0.5 * (conserved[5] * conserved[5] + conserved[6] * conserved[6] + conserved[7] * conserved[7])
    pressure = (GAMMA - 1.0) * (conserved[4] - kinetic - magnetic)
    return jnp.stack([density, vel_r, vel_t, vel_z, pressure, conserved[5], conserved[6], conserved[7]])

def physical(states, normal):
    density = states[0]
    velocity = (states[1], states[2], states[3])
    pressure = states[4]
    field = (states[5], states[6], states[7])
    vel_n = velocity[normal]
    field_n = field[normal]
    field_sq = field[0] * field[0] + field[1] * field[1] + field[2] * field[2]
    speed_sq = velocity[0] * velocity[0] + velocity[1] * velocity[1] + velocity[2] * velocity[2]
    vel_dot = velocity[0] * field[0] + velocity[1] * field[1] + velocity[2] * field[2]
    total_p = pressure + 0.5 * field_sq
    energy = pressure / (GAMMA - 1.0) + 0.5 * density * speed_sq + 0.5 * field_sq
    conserved = jnp.stack([density, density * velocity[0], density * velocity[1], density * velocity[2], energy, field[0], field[1], field[2]])
    momentum = [density * velocity[component] * vel_n - field[component] * field_n + (total_p if component == normal else 0.0) for component in (0, 1, 2)]
    induction = [vel_n * field[component] - field_n * velocity[component] for component in (0, 1, 2)]
    fluxes = jnp.stack([density * vel_n] + momentum + [(energy + total_p) * vel_n - field_n * vel_dot] + induction)
    signal = jnp.abs(vel_n) + jnp.sqrt((GAMMA * pressure + field_sq) / density)
    return (conserved, fluxes, signal)

def rusanov(left_state, right_state, normal):
    cons_left, flux_left, signal_left = physical(left_state, normal)
    cons_right, flux_right, signal_right = physical(right_state, normal)
    return 0.5 * (flux_left + flux_right) - 0.5 * jnp.maximum(signal_left, signal_right) * (cons_right - cons_left)

def minmod(lower_diff, upper_diff):
    return 0.5 * (jnp.sign(lower_diff) + jnp.sign(upper_diff)) * jnp.minimum(jnp.abs(lower_diff), jnp.abs(upper_diff))

def face_pairs(extended, axis_dim, length):
    middle = lax.slice_in_dim(extended, 1, length + 3, axis=axis_dim)
    behind = lax.slice_in_dim(extended, 0, length + 2, axis=axis_dim)
    beyond = lax.slice_in_dim(extended, 2, length + 4, axis=axis_dim)
    slopes = minmod(middle - behind, beyond - middle)
    left_state = lax.slice_in_dim(middle + 0.5 * slopes, 0, length + 1, axis=axis_dim)
    right_state = lax.slice_in_dim(middle - 0.5 * slopes, 1, length + 2, axis=axis_dim)
    return (left_state, right_state)

def local_residual(conserved, theta_ext, axial_ext, partner_row, dtheta):
    fields, depth_z, width_t, radial = conserved.shape
    states = primitive(conserved)
    theta_states = jnp.concatenate([primitive(theta_ext[:, :, :2]), states, primitive(theta_ext[:, :, -2:])], axis=2)
    axial_states = jnp.concatenate([primitive(axial_ext[:, :2]), states, primitive(axial_ext[:, -2:])], axis=1)
    flipper = jnp.array(AXIS_FLIP, jnp.float32).reshape(-1, 1, 1)
    across = primitive(partner_row) * flipper
    behind = jnp.concatenate([across[..., None], states[..., :-1]], axis=-1)
    beyond = jnp.concatenate([states[..., 1:], states[..., -1:]], axis=-1)
    slopes = minmod(states - behind, beyond - states)
    left_state = states + 0.5 * slopes
    right_state = jnp.concatenate([(states - 0.5 * slopes)[..., 1:], states[..., -1:]], axis=-1)
    radial_flux = rusanov(left_state, right_state, 0)
    face_radius = jnp.arange(radial, dtype=jnp.float32) + 1.0
    cell_radius = jnp.arange(radial, dtype=jnp.float32) + 0.5
    outward = radial_flux * (face_radius * dtheta)
    inward = jnp.concatenate([jnp.zeros_like(outward[..., :1]), outward[..., :-1]], axis=-1)
    theta_left, theta_right = face_pairs(theta_states, 2, width_t)
    theta_flux = rusanov(theta_left, theta_right, 1)
    axial_left, axial_right = face_pairs(axial_states, 1, depth_z)
    axial_flux = rusanov(axial_left, axial_right, 2)
    residual = inward - outward - (theta_flux[:, :, 1:] - theta_flux[:, :, :-1]) - (axial_flux[:, 1:] - axial_flux[:, :-1]) * (cell_radius * dtheta)
    density = states[0]
    vel_r = states[1]
    vel_t = states[2]
    pressure = states[4]
    field_r = states[5]
    field_t = states[6]
    field_sq = states[5] * states[5] + states[6] * states[6] + states[7] * states[7]
    residual = residual.at[1].add(dtheta * (density * vel_t * vel_t + pressure + 0.5 * field_sq - field_t * field_t))
    residual = residual.at[2].add(-dtheta * (density * vel_r * vel_t - field_r * field_t))
    residual = residual.at[6].add(dtheta * (vel_r * field_t - vel_t * field_r))
    return (residual, radial_flux)

def reflux(residual, radial_flux, fine_cells, face_index, dtheta):
    radial = residual.shape[-1]
    positions = jnp.arange(radial, dtype=jnp.int32)
    pick_face = (positions[None, :] == (face_index - 1)[:, None]).astype(jnp.float32)
    coarse_face = lax.optimization_barrier(jnp.sum(radial_flux * pick_face, axis=-1))
    mismatch = fine_cells - coarse_face
    area = face_index.astype(jnp.float32) * dtheta
    correction = area * mismatch
    outer_cell = (positions[None, :] == face_index[:, None]).astype(jnp.float32)
    volume = (jnp.arange(radial, dtype=jnp.float32) + 0.5) * dtheta
    return ((residual + correction[..., None] * outer_cell) / volume, mismatch)

def fine_faces(fine_rim):
    rim_states = jnp.moveaxis(fine_rim, 2, 0)
    flux_out = rusanov(rim_states[:, :, 0], rim_states[:, :, 1], 0)
    fields, slot_total, length = flux_out.shape
    paired = flux_out.reshape(fields, slot_total, length // (2 * BT), BT, 2)
    return 0.25 * lax.optimization_barrier(jnp.sum(paired, axis=-1))

def reference(fluid_state, levels, fine_rim, slot_owner, slot_block, slot_count):
    dtheta = 2.0 * math.pi / NT
    padded = jnp.pad(fluid_state, ((0, 0), (2, 2), (0, 0), (0, 0)), mode='edge')
    partner = jnp.roll(fluid_state[..., 0], NT // 2, axis=2)
    partials = fine_faces(fine_rim)
    slot_ids = jnp.arange(SLOT_ALL, dtype=jnp.int32)
    live_slots = slot_ids % SLOTS < slot_count[slot_ids // SLOTS]
    target = slot_owner * (CT // BT) + slot_block
    chosen = ((jnp.arange(NTB, dtype=jnp.int32)[:, None] == target[None, :]) & live_slots[None, :]).astype(jnp.float32)
    registers = jnp.einsum('gs,fszb->fzgb', chosen, partials, precision=lax.Precision.HIGHEST).reshape(FIELDS, NZ, NT)
    face_index = jnp.repeat(BR * lax.optimization_barrier(jnp.sum(levels, axis=0)), BT).astype(jnp.int32)

    def one_block(block_id):
        first_z = block_id * CZ
        conserved = lax.dynamic_slice_in_dim(fluid_state, first_z, CZ, axis=1)
        axial_ext = lax.dynamic_slice_in_dim(padded, first_z, CZ + 4, axis=1)
        theta_ext = jnp.concatenate([conserved[:, :, -2:], conserved, conserved[:, :, :2]], axis=2)
        partner_row = lax.dynamic_slice_in_dim(partner, first_z, CZ, axis=1)
        fine_cells = lax.dynamic_slice_in_dim(registers, first_z, CZ, axis=1)
        residual, radial_flux = local_residual(conserved, theta_ext, axial_ext, partner_row, dtheta)
        result, mismatch = reflux(residual, radial_flux, fine_cells, face_index, dtheta)
        return (result, mismatch, radial_flux[..., 0])
    blocks, mismatches, inners = lax.map(one_block, jnp.arange(NZ // CZ, dtype=jnp.int32))
    residual = jnp.moveaxis(blocks, 0, 1).reshape(FIELDS, NZ, NT, NR)
    flux_mismatch = jnp.moveaxis(mismatches, 0, 1).reshape(FIELDS, NZ, NT)
    inner_flux = jnp.moveaxis(inners, 0, 1).reshape(FIELDS, NZ, NT)
    return (residual, flux_mismatch, inner_flux)
```

```python
import functools
import math

import jax
import jax.numpy as jnp
from jax import lax
from jax.experimental import pallas as pl
from jax.experimental.pallas import tpu as pltpu
from jax.sharding import PartitionSpec as P

BT = 8
BR = 32
GAMMA = 5.0 / 3.0
FLIPPED = (1, 2, 5, 6)
QUAD = 4
F32 = jnp.float32
MESH = pl.DeviceIdType.MESH


def primitive(cons):
    rho, mr, mt, mz, energy, br, bt, bz = cons
    inv = 1.0 / rho
    vr, vt, vz = mr * inv, mt * inv, mz * inv
    kinetic = mr * vr + mt * vt + mz * vz
    magnetic = br * br + bt * bt + bz * bz
    pressure = (GAMMA - 1.0) * (energy - 0.5 * (kinetic + magnetic))
    return [rho, vr, vt, vz, pressure, br, bt, bz]


def side_state(state, normal):
    rho, pressure = state[0], state[4]
    vel, field = state[1:4], state[5:8]
    mom = [rho * v for v in vel]
    vel_n, field_n = vel[normal], field[normal]
    field_sq = field[0] * field[0] + field[1] * field[1] + field[2] * field[2]
    half_sq = 0.5 * field_sq
    kinetic = 0.5 * (mom[0] * vel[0] + mom[1] * vel[1] + mom[2] * vel[2])
    vel_dot = vel[0] * field[0] + vel[1] * field[1] + vel[2] * field[2]
    total_p = pressure + half_sq
    energy = pressure * (1.0 / (GAMMA - 1.0)) + kinetic + half_sq
    flux = [mom[normal]]
    for comp in range(3):
        term = mom[comp] * vel_n - field[comp] * field_n
        flux.append(term + total_p if comp == normal else term)
    flux.append((energy + total_p) * vel_n - field_n * vel_dot)
    for comp in range(3):
        flux.append(None if comp == normal else vel_n * field[comp] - field_n * vel[comp])
    fast = GAMMA * pressure + field_sq
    signal = jnp.abs(vel_n) + fast * lax.rsqrt(fast * rho)
    return [rho] + mom + [energy] + list(field), flux, signal


def double_flux(left, right, normal):
    cons_l, flux_l, signal_l = side_state(left, normal)
    cons_r, flux_r, signal_r = side_state(right, normal)
    top = jnp.maximum(signal_l, signal_r)
    out = []
    for ul, ur, fl, fr in zip(cons_l, cons_r, flux_l, flux_r):
        if fl is None:
            out.append(top * (ul - ur))
        else:
            out.append((fl + fr) - top * (ur - ul))
    return out


def half_slope(lower, upper):
    low, high = jnp.minimum(lower, upper), jnp.maximum(lower, upper)
    return 0.5 * (jnp.maximum(low, 0.0) + jnp.minimum(high, 0.0))


def kernel(
    sizes,
    x_hbm, fine_hbm, levels_hbm, owner_hbm, block_hbm, count_hbm,
    res_ref, mis_ref, inner_ref,
    x_v, fine_v, prim_v, cross_v, edge_v, edge_in, packed_v, turned_v, corr_v,
    quad_v, out_v, in_v,
    levels_s, owner_s, block_s, count_s,
    load_sem, quad_send, quad_recv, ring_send, ring_recv, halo_send, halo_recv,
):
    theta_n, gz_n, depth, width, dtheta = sizes
    rows = depth * width
    ring_n = theta_n // QUAD
    theta = lax.axis_index("theta")
    gz = lax.axis_index("gz")
    ring_pos, quad_pos = theta // QUAD, theta % QUAD

    def load(src, dst, sem):
        return pltpu.make_async_copy(src, dst, load_sem.at[sem])

    loads = [
        load(fine_hbm, fine_v, 0),
        load(x_hbm, x_v, 1),
        load(levels_hbm, levels_s, 2),
        load(owner_hbm, owner_s, 3),
        load(block_hbm, block_s, 4),
        load(count_hbm, count_s, 5),
    ]
    for item in loads:
        item.start()

    barrier = pltpu.get_barrier_semaphore()
    greeted = 0

    def greet(t, g):
        pl.semaphore_signal(barrier, inc=1, device_id={"theta": t, "gz": g}, device_id_type=MESH)

    ring_steps = sorted(range(1, ring_n), key=lambda d: -min(d, ring_n - d))
    for step in ring_steps:
        greet((ring_pos + step) % ring_n * QUAD + quad_pos, gz)
        greeted += 1
    for t, g in (
        ((theta + 1) % theta_n, gz),
        ((theta + theta_n - 1) % theta_n, gz),
        (theta, (gz + 1) % gz_n),
        (theta, (gz + gz_n - 1) % gz_n),
    ):
        greet(t, g)
        greeted += 1
    for step in range(1, QUAD):
        greet(ring_pos * QUAD + (quad_pos + step) % QUAD, gz)
        greeted += 1

    lane = lax.broadcasted_iota(jnp.int32, (8, 128), 1)
    lane_block = (lane % width) // BT

    loads[0].wait()
    sides = [
        [fine_v[pl.ds(side * 8 + var, 8, stride=16), :] for var in range(8)] for side in (0, 1)
    ]
    fine_flux = jnp.concatenate(double_flux(sides[0], sides[1], 0), axis=0)
    src = lax.broadcasted_iota(jnp.int32, (128, 128), 0)
    dst = lax.broadcasted_iota(jnp.int32, (128, 128), 1)
    pairing = jnp.where(
        (src // width == dst // width) & ((src % width) // 2 == dst % BT), 0.125, 0.0
    ).astype(F32)
    partial = jnp.dot(
        fine_flux, pairing, precision=lax.Precision.HIGHEST, preferred_element_type=F32
    )
    for var in range(8):
        quad_v[quad_pos, pl.ds(var, 8, stride=8), :] = partial[var * 8 : var * 8 + 8]

    loads[1].wait()

    def to_primitive(step, edge):
        z = depth - 1 - step
        at = pl.multiple_of(z * width, width)
        edge = pltpu.roll(edge, width, 1)
        for half in range(2):
            prims = primitive([x_v[f, pl.ds(at + half * 8, 8), :] for f in range(8)])
            for f, value in enumerate(prims):
                prim_v[f, pl.ds(at + 2 * width + half * 8, 8), :] = value
                cross_v[f, pl.ds((2 + half * 8) * depth + z, 8, stride=depth), :] = value
                place = half * 8 + f
                moved = pltpu.roll(value, place, 1) if place else value
                edge = jnp.where(lane == place, -moved if f in FLIPPED else moved, edge)
        return edge

    edge_v[...] = lax.fori_loop(0, depth, to_primitive, jnp.zeros((8, 128), F32))

    for item in loads[2:]:
        item.wait()
    pl.semaphore_wait(barrier, greeted)

    def remote(src, dst, send, recv, t, g):
        return pltpu.make_async_remote_copy(
            src_ref=src, dst_ref=dst, send_sem=send, recv_sem=recv,
            device_id={"theta": t, "gz": g}, device_id_type=MESH,
        )

    across = remote(
        edge_v, edge_in, halo_send.at[0], halo_recv.at[0], (theta + theta_n // 2) % theta_n, gz
    )
    across.start()
    quad_copies = []
    for step in range(1, QUAD):
        copy = remote(
            quad_v.at[quad_pos], quad_v.at[quad_pos], quad_send.at[step], quad_recv.at[step],
            ring_pos * QUAD + (quad_pos + step) % QUAD, gz,
        )
        copy.start()
        quad_copies.append(copy)
    two_z, two_t = 2 * width, 2 * depth
    up = remote(
        prim_v.at[:, pl.ds(rows, two_z)], prim_v.at[:, pl.ds(0, two_z)],
        halo_send.at[1], halo_recv.at[1], theta, (gz + 1) % gz_n,
    )
    down = remote(
        prim_v.at[:, pl.ds(two_z, two_z)], prim_v.at[:, pl.ds(rows + two_z, two_z)],
        halo_send.at[2], halo_recv.at[2], theta, (gz + gz_n - 1) % gz_n,
    )
    not_last, not_first = gz < gz_n - 1, gz > 0
    pl.when(not_last)(up.start)
    pl.when(not_first)(down.start)
    ahead = remote(
        cross_v.at[:, pl.ds(rows, two_t)], cross_v.at[:, pl.ds(0, two_t)],
        halo_send.at[3], halo_recv.at[3], (theta + 1) % theta_n, gz,
    )
    back = remote(
        cross_v.at[:, pl.ds(two_t, two_t)], cross_v.at[:, pl.ds(rows + two_t, two_t)],
        halo_send.at[4], halo_recv.at[4], (theta + theta_n - 1) % theta_n, gz,
    )
    ahead.start()
    back.start()

    @pl.when(gz == 0)
    def _():
        for f in range(8):
            plane = prim_v[f, pl.ds(two_z, width), :]
            prim_v[f, pl.ds(0, width), :] = plane
            prim_v[f, pl.ds(width, width), :] = plane

    @pl.when(gz == gz_n - 1)
    def _():
        for f in range(8):
            plane = prim_v[f, pl.ds(rows + width, width), :]
            prim_v[f, pl.ds(rows + 2 * width, width), :] = plane
            prim_v[f, pl.ds(rows + 3 * width, width), :] = plane

    radius = lane.astype(F32) + 0.5
    inv_radius = 1.0 / radius
    inward = 0.5 * (radius - 0.5) * inv_radius
    outward = 0.5 * (radius + 0.5) * inv_radius
    turn = inv_radius * (0.5 / dtheta)
    pick = jnp.where(lane < 16, lane - 1, lane % BR)
    first, last = lane == 0, lane == 127

    across.wait()

    def radial(z, edge):
        at = pl.multiple_of(z * width, width)
        for half in range(2):
            left, right = [], []
            cell = [prim_v[f, pl.ds(at + two_z + half * 8, 8), :] for f in range(8)]
            for f in range(8):
                mid = cell[f]
                place = half * 8 + f
                inner = pltpu.roll(edge, 128 - place, 1) if place else edge
                lower = mid - jnp.where(first, inner, pltpu.roll(mid, 1, 1))
                upper = jnp.where(last, 0.0, pltpu.roll(lower, 127, 1))
                slope = half_slope(lower, upper)
                left.append(mid + slope)
                right.append(jnp.where(last, mid, pltpu.roll(mid - slope, 127, 1)))
            flux = double_flux(left, right, 0)
            rho, vr, vt, _, pressure, br, bt, bz = cell
            out = [inward * pltpu.roll(v, 1, 1) - outward * v for v in flux]
            field_sq = br * br + bt * bt + bz * bz
            out[1] = out[1] + inv_radius * (rho * vt * vt + pressure + 0.5 * field_sq - bt * bt)
            out[2] = out[2] - inv_radius * (rho * vr * vt - br * bt)
            out[6] = out[6] + inv_radius * (vr * bt - vt * br)
            packed = jnp.zeros((8, 128), F32)
            for f in range(8):
                res_ref[f, pl.ds(at + half * 8, 8), :] = out[f]
                packed = jnp.where(pick == f, pltpu.roll(flux[f], f + 1, 1), packed)
            packed_v[pl.ds(at + half * 8, 8), :] = packed
        return pltpu.roll(edge, 128 - width, 1)

    lax.fori_loop(0, depth, radial, edge_in[...])

    for copy in quad_copies:
        copy.wait()

    def spread(slot, totals):
        index = ring_pos * (QUAD * 8) + slot
        live = slot % 8 < count_s[ring_pos * QUAD + slot // 8]
        code = jnp.where(live, owner_s[index] * 2 + block_s[index], -1)
        relative = code - 2 * quad_pos - lane_block
        value = quad_v[slot // 8, pl.ds(pl.multiple_of(slot % 8 * 8, 8), 8), :]
        return tuple(
            total + jnp.where(relative == 2 * QUAD * k, value, 0.0)
            for k, total in enumerate(totals)
        )

    totals = lax.fori_loop(
        0, QUAD * 8, spread, tuple(jnp.zeros((8, 128), F32) for _ in range(ring_n))
    )
    for k in range(ring_n):
        out_v[k] = totals[k]
    ring_copies = []
    for step in ring_steps:
        to = (ring_pos + step) % ring_n
        copy = remote(
            out_v.at[to], in_v.at[ring_pos], ring_send.at[step], ring_recv.at[step],
            to * QUAD + quad_pos, gz,
        )
        copy.start()
        ring_copies.append(copy)

    def sweep(load_plane, faces, normal, emit):
        before, cell = load_plane(0), load_plane(1)
        after = load_plane(2)
        diff = [b - a for a, b in zip(before, cell)]
        diff_up = [b - a for a, b in zip(cell, after)]
        left = [c + half_slope(a, b) for a, b, c in zip(diff, diff_up, cell)]

        def face(k, carry):
            cell, diff, left, flux_low = carry
            after = load_plane(k + 3)
            diff_up = [b - a for a, b in zip(cell, after)]
            slope = [half_slope(a, b) for a, b in zip(diff, diff_up)]
            right = [c - s for c, s in zip(cell, slope)]
            flux = double_flux(left, right, normal)
            return after, diff_up, [c + s for c, s in zip(cell, slope)], flux

        carry = face(0, (after, diff_up, left, None))

        def body(k, carry):
            low = carry[3]
            carry = face(k, carry)
            emit(k - 1, [b - a for a, b in zip(low, carry[3])])
            return carry

        lax.fori_loop(1, faces, body, carry)

    ahead.wait()
    back.wait()

    def theta_plane(k):
        return [cross_v[f, pl.ds(pl.multiple_of(k * depth, depth), depth), :] for f in range(8)]

    def theta_emit(k, change):
        for f in range(8):
            at = pl.ds(k, depth, stride=width)
            res_ref[f, at, :] = res_ref[f, at, :] - turn * change[f]

    sweep(theta_plane, width + 1, 1, theta_emit)

    depth_of = [levels_s[b, 0] + levels_s[b, 1] + levels_s[b, 2] + levels_s[b, 3] for b in range(2)]
    turned_v[...] = packed_v[...].T
    for copy in ring_copies:
        copy.wait()
    registers = out_v[ring_pos]
    for step in range(1, ring_n):
        registers = registers + in_v[(ring_pos + step) % ring_n]
    level = jnp.where(lane_block == 0, depth_of[0], depth_of[1])
    coarse = jnp.where(
        level == 1,
        turned_v[BR : BR + 8, :],
        jnp.where(level == 2, turned_v[2 * BR : 2 * BR + 8, :], turned_v[3 * BR : 3 * BR + 8, :]),
    )
    mismatch = registers - 0.5 * coarse
    inner = 0.5 * turned_v[1:9, :]
    for z in range(depth):
        shift = (128 - z * width) % 128
        at = pl.ds(z, 8, stride=depth)
        mis_ref[at, :] = (pltpu.roll(mismatch, shift, 1) if shift else mismatch)[:, :width]
        inner_ref[at, :] = (pltpu.roll(inner, shift, 1) if shift else inner)[:, :width]
    face = (BR * level).astype(F32)
    corr_v[...] = jnp.concatenate([mismatch * (face / (face + 0.5))] * 16, axis=0).T

    @pl.when(not_first)
    def _():
        up.wait_recv()
        down.wait_send()

    @pl.when(not_last)
    def _():
        up.wait_send()
        down.wait_recv()

    for half in range(2):
        hit = lane == BR * depth_of[half]

        def axial_plane(k):
            at = pl.multiple_of(k * width + half * 8, 8)
            return [prim_v[f, pl.ds(at, 8), :] for f in range(8)]

        def axial_emit(k, change):
            at = pl.ds(pl.multiple_of(k * width + half * 8, 8), 8)
            corr = corr_v[at, :]
            for f in range(8):
                moved = pltpu.roll(corr, 128 - f, 1) if f else corr
                res_ref[f, at, :] = (
                    res_ref[f, at, :] - 0.5 * change[f] + jnp.where(hit, moved, 0.0)
                )

        sweep(axial_plane, depth + 1, 2, axial_emit)


def body(mesh_shape, fluid_state, levels, fine_rim, slot_owner, slot_block, slot_count):
    fields, depth, width, radial = fluid_state.shape
    theta_n, gz_n = mesh_shape
    rows = depth * width
    ring_n = theta_n // QUAD
    slots = fine_rim.shape[0]
    sizes = (theta_n, gz_n, depth, width, 2.0 * math.pi / (width * theta_n))
    hbm = pl.BlockSpec(memory_space=pltpu.MemorySpace.HBM)
    vmem = pl.BlockSpec(memory_space=pltpu.MemorySpace.VMEM)
    res, mis, inner = pl.pallas_call(
        functools.partial(kernel, sizes),
        out_shape=(
            jax.ShapeDtypeStruct((fields, rows, radial), F32),
            jax.ShapeDtypeStruct((fields * depth, width), F32),
            jax.ShapeDtypeStruct((fields * depth, width), F32),
        ),
        in_specs=[hbm] * 6,
        out_specs=(vmem, vmem, vmem),
        scratch_shapes=[
            pltpu.VMEM((fields, rows, radial), F32),
            pltpu.VMEM((slots * 2 * fields, 128), F32),
            pltpu.VMEM((fields, rows + 4 * width, radial), F32),
            pltpu.VMEM((fields, rows + 4 * depth, radial), F32),
            pltpu.VMEM((8, 128), F32),
            pltpu.VMEM((8, 128), F32),
            pltpu.VMEM((rows, 128), F32),
            pltpu.VMEM((128, rows), F32),
            pltpu.VMEM((rows, 128), F32),
            pltpu.VMEM((QUAD, slots * fields, 128), F32),
            pltpu.VMEM((ring_n, 8, 128), F32),
            pltpu.VMEM((ring_n, 8, 128), F32),
            pltpu.SMEM((2, 4), jnp.int32),
            pltpu.SMEM(slot_owner.shape, jnp.int32),
            pltpu.SMEM(slot_block.shape, jnp.int32),
            pltpu.SMEM(slot_count.shape, jnp.int32),
            pltpu.SemaphoreType.DMA((6,)),
            pltpu.SemaphoreType.DMA((QUAD,)),
            pltpu.SemaphoreType.DMA((QUAD,)),
            pltpu.SemaphoreType.DMA((ring_n,)),
            pltpu.SemaphoreType.DMA((ring_n,)),
            pltpu.SemaphoreType.DMA((5,)),
            pltpu.SemaphoreType.DMA((5,)),
        ],
        compiler_params=pltpu.CompilerParams(
            collective_id=0, has_side_effects=True, vmem_limit_bytes=32 * 1024 * 1024
        ),
    )(
        fluid_state.reshape(fields, rows, radial),
        fine_rim.reshape(slots * 2 * fields, 128),
        levels.T,
        slot_owner,
        slot_block,
        slot_count,
    )
    return (
        res.reshape(fields, depth, width, radial),
        mis.reshape(fields, depth, width),
        inner.reshape(fields, depth, width),
    )


def solution(mesh):
    return jax.shard_map(
        functools.partial(body, (mesh.shape["theta"], mesh.shape["gz"])),
        mesh=mesh,
        in_specs=(
            P(None, "gz", "theta", None),
            P(None, "theta"),
            P("theta", None, None, "gz"),
            P(),
            P(),
            P(),
        ),
        out_specs=(P(None, "gz", "theta", None), P(None, "gz", "theta"), P(None, "gz", "theta")),
        check_vma=False,
    )
```

```python
import functools
import math

import jax
import jax.numpy as jnp
from jax import lax
from jax.experimental import pallas as pl
from jax.experimental.pallas import tpu as pltpu
from jax.sharding import PartitionSpec as P

BT = 8
BR = 32
GAMMA = 5.0 / 3.0
QUAD = 4
F32 = jnp.float32
MESH = pl.DeviceIdType.MESH


def primitive(cons):
    rho, mr, mt, mz, energy, br, bt, bz = cons
    inv = 1.0 / rho
    vr, vt, vz = mr * inv, mt * inv, mz * inv
    kinetic = mr * vr + mt * vt + mz * vz
    magnetic = br * br + bt * bt + bz * bz
    pressure = (GAMMA - 1.0) * (energy - 0.5 * (kinetic + magnetic))
    return [rho, vr, vt, vz, pressure, br, bt, bz]


def side_state(state, normal):
    rho, pressure = state[0], state[4]
    vel, field = state[1:4], state[5:8]
    mom = [rho * v for v in vel]
    vel_n, field_n = vel[normal], field[normal]
    field_sq = field[0] * field[0] + field[1] * field[1] + field[2] * field[2]
    half_sq = 0.5 * field_sq
    kinetic = 0.5 * (mom[0] * vel[0] + mom[1] * vel[1] + mom[2] * vel[2])
    vel_dot = vel[0] * field[0] + vel[1] * field[1] + vel[2] * field[2]
    total_p = pressure + half_sq
    energy = pressure * (1.0 / (GAMMA - 1.0)) + kinetic + half_sq
    flux = [mom[normal]]
    for comp in range(3):
        term = mom[comp] * vel_n - field[comp] * field_n
        flux.append(term + total_p if comp == normal else term)
    flux.append((energy + total_p) * vel_n - field_n * vel_dot)
    for comp in range(3):
        flux.append(None if comp == normal else vel_n * field[comp] - field_n * vel[comp])
    fast = GAMMA * pressure + field_sq
    signal = jnp.abs(vel_n) + fast * lax.rsqrt(fast * rho)
    return [rho] + mom + [energy] + list(field), flux, signal


def double_flux(left, right, normal):
    cons_l, flux_l, signal_l = side_state(left, normal)
    cons_r, flux_r, signal_r = side_state(right, normal)
    top = jnp.maximum(signal_l, signal_r)
    out = []
    for ul, ur, fl, fr in zip(cons_l, cons_r, flux_l, flux_r):
        if fl is None:
            out.append(top * (ul - ur))
        else:
            out.append((fl + fr) - top * (ur - ul))
    return out


def half_slope(lower, upper):
    low, high = jnp.minimum(lower, upper), jnp.maximum(lower, upper)
    return 0.5 * (jnp.maximum(low, 0.0) + jnp.minimum(high, 0.0))


def kernel(
    sizes,
    x_hbm, fine_hbm, levels_hbm, owner_hbm, block_hbm, count_hbm,
    res_ref, mis_ref, inner_ref,
    x_v, fine_v, prim_v, cross_v, edge_v, edge_in, packed_v, turned_v, corr_v,
    quad_v, out_v, in_v,
    levels_s, owner_s, block_s, count_s,
    load_sem, quad_send, quad_recv, ring_send, ring_recv, halo_send, halo_recv,
):
    theta_n, gz_n, depth, width, dtheta = sizes
    rows = depth * width
    ring_n = theta_n // QUAD
    theta = lax.axis_index("theta")
    gz = lax.axis_index("gz")
    ring_pos, quad_pos = theta // QUAD, theta % QUAD

    def load(src, dst, sem):
        return pltpu.make_async_copy(src, dst, load_sem.at[sem])

    loads = [
        load(fine_hbm, fine_v, 0),
        load(x_hbm, x_v, 1),
        load(levels_hbm, levels_s, 2),
        load(owner_hbm, owner_s, 3),
        load(block_hbm, block_s, 4),
        load(count_hbm, count_s, 5),
    ]
    for item in loads:
        item.start()

    barrier = pltpu.get_barrier_semaphore()
    greeted = 0

    def greet(t, g):
        pl.semaphore_signal(barrier, inc=1, device_id={"theta": t, "gz": g}, device_id_type=MESH)

    ring_steps = sorted(range(1, ring_n), key=lambda d: -min(d, ring_n - d))
    for step in ring_steps:
        greet((ring_pos + step) % ring_n * QUAD + quad_pos, gz)
        greeted += 1
    for t, g in (
        ((theta + 1) % theta_n, gz),
        ((theta + theta_n - 1) % theta_n, gz),
        (theta, (gz + 1) % gz_n),
        (theta, (gz + gz_n - 1) % gz_n),
    ):
        greet(t, g)
        greeted += 1
    for step in range(1, QUAD):
        greet(ring_pos * QUAD + (quad_pos + step) % QUAD, gz)
        greeted += 1

    lane = lax.broadcasted_iota(jnp.int32, (8, 128), 1)
    lane_block = (lane % width) // BT

    loads[0].wait()
    sides = [
        [fine_v[pl.ds(side * 8 + var, 8, stride=16), :] for var in range(8)] for side in (0, 1)
    ]
    fine_flux = jnp.concatenate(double_flux(sides[0], sides[1], 0), axis=0)
    src = lax.broadcasted_iota(jnp.int32, (128, 128), 0)
    dst = lax.broadcasted_iota(jnp.int32, (128, 128), 1)
    pairing = jnp.where(
        (src // width == dst // width) & ((src % width) // 2 == dst % BT), 0.125, 0.0
    ).astype(F32)
    partial = jnp.dot(
        fine_flux, pairing, precision=lax.Precision.HIGHEST, preferred_element_type=F32
    )
    for var in range(8):
        quad_v[quad_pos, pl.ds(var, 8, stride=8), :] = partial[var * 8 : var * 8 + 8]

    loads[1].wait()

    def to_primitive(z, _):
        at = pl.multiple_of(z * width, width)
        for half in range(2):
            prims = primitive([x_v[f, pl.ds(at + half * 8, 8), :] for f in range(8)])
            for f, value in enumerate(prims):
                prim_v[f, pl.ds(at + 2 * width + half * 8, 8), :] = value
                cross_v[f, pl.ds((2 + half * 8) * depth + z, 8, stride=depth), :] = value
        return 0

    lax.fori_loop(0, depth, to_primitive, 0)

    for item in loads[2:]:
        item.wait()

    radius = lane.astype(F32) + 0.5
    inv_radius = 1.0 / radius
    inward = jnp.where(lane == 1, 0.0, 0.5 * (radius - 0.5) * inv_radius)
    outward = jnp.where(lane == 0, 0.0, 0.5 * (radius + 0.5) * inv_radius)
    turn = inv_radius * (0.5 / dtheta)
    last = lane == 127
    spot = jnp.where(lane >= BR, lane % BR, -1)

    def radial(z, _):
        for half in range(2):
            at = pl.multiple_of(z * width + half * 8, 8)
            left, right = [], []
            cell = [prim_v[f, pl.ds(at + 2 * width, 8), :] for f in range(8)]
            packed = jnp.zeros((8, 128), F32)
            for f in range(8):
                mid = cell[f]
                lower = mid - pltpu.roll(mid, 1, 1)
                upper = jnp.where(last, 0.0, pltpu.roll(lower, 127, 1))
                slope = half_slope(lower, upper)
                left.append(mid + slope)
                right.append(jnp.where(last, mid, pltpu.roll(mid - slope, 127, 1)))
                packed = jnp.where(lane == f, pltpu.roll(mid, f, 1) if f else mid, packed)
                packed = jnp.where(lane == f + 8, pltpu.roll(upper, f + 8, 1), packed)
                packed = jnp.where(lane == f + 16, pltpu.roll(right[f], f + 16, 1), packed)
            flux = double_flux(left, right, 0)
            rho, vr, vt, _, pressure, br, bt, bz = cell
            out = [inward * pltpu.roll(v, 1, 1) - outward * v for v in flux]
            field_sq = br * br + bt * bt + bz * bz
            out[1] = out[1] + inv_radius * (rho * vt * vt + pressure + 0.5 * field_sq - bt * bt)
            out[2] = out[2] - inv_radius * (rho * vr * vt - br * bt)
            out[6] = out[6] + inv_radius * (vr * bt - vt * br)
            for f in range(8):
                res_ref[f, pl.ds(at, 8), :] = out[f]
                packed = jnp.where(spot == f, pltpu.roll(flux[f], f + 1, 1), packed)
            packed_v[pl.ds(at, 8), :] = packed
        return 0

    lax.fori_loop(0, depth, radial, 0)
    turned_v[...] = packed_v[...].T
    row = lax.broadcasted_iota(jnp.int32, (8, 128), 0)
    flip = (row == 1) | (row == 2) | (row == 5) | (row == 6)
    edge_v[...] = jnp.where(flip, -turned_v[0:8, :], turned_v[0:8, :])

    depth_of = [levels_s[b, 0] + levels_s[b, 1] + levels_s[b, 2] + levels_s[b, 3] for b in range(2)]
    level = jnp.where(lane_block == 0, depth_of[0], depth_of[1])
    coarse = 0.5 * jnp.where(
        level == 1,
        turned_v[BR : BR + 8, :],
        jnp.where(level == 2, turned_v[2 * BR : 2 * BR + 8, :], turned_v[3 * BR : 3 * BR + 8, :]),
    )

    pl.semaphore_wait(barrier, greeted)

    def remote(src, dst, send, recv, t, g):
        return pltpu.make_async_remote_copy(
            src_ref=src, dst_ref=dst, send_sem=send, recv_sem=recv,
            device_id={"theta": t, "gz": g}, device_id_type=MESH,
        )

    quad_copies = []
    for step in range(1, QUAD):
        copy = remote(
            quad_v.at[quad_pos], quad_v.at[quad_pos], quad_send.at[step], quad_recv.at[step],
            ring_pos * QUAD + (quad_pos + step) % QUAD, gz,
        )
        copy.start()
        quad_copies.append(copy)
    across = remote(
        edge_v, edge_in, halo_send.at[0], halo_recv.at[0], (theta + theta_n // 2) % theta_n, gz
    )
    across.start()
    two_z, two_t = 2 * width, 2 * depth
    up = remote(
        prim_v.at[:, pl.ds(rows, two_z)], prim_v.at[:, pl.ds(0, two_z)],
        halo_send.at[1], halo_recv.at[1], theta, (gz + 1) % gz_n,
    )
    down = remote(
        prim_v.at[:, pl.ds(two_z, two_z)], prim_v.at[:, pl.ds(rows + two_z, two_z)],
        halo_send.at[2], halo_recv.at[2], theta, (gz + gz_n - 1) % gz_n,
    )
    not_last, not_first = gz < gz_n - 1, gz > 0
    pl.when(not_last)(up.start)
    pl.when(not_first)(down.start)
    ahead = remote(
        cross_v.at[:, pl.ds(rows, two_t)], cross_v.at[:, pl.ds(0, two_t)],
        halo_send.at[3], halo_recv.at[3], (theta + 1) % theta_n, gz,
    )
    back = remote(
        cross_v.at[:, pl.ds(two_t, two_t)], cross_v.at[:, pl.ds(rows + two_t, two_t)],
        halo_send.at[4], halo_recv.at[4], (theta + theta_n - 1) % theta_n, gz,
    )
    ahead.start()
    back.start()

    @pl.when(gz == 0)
    def _():
        for f in range(8):
            plane = prim_v[f, pl.ds(two_z, width), :]
            prim_v[f, pl.ds(0, width), :] = plane
            prim_v[f, pl.ds(width, width), :] = plane

    @pl.when(gz == gz_n - 1)
    def _():
        for f in range(8):
            plane = prim_v[f, pl.ds(rows + width, width), :]
            prim_v[f, pl.ds(rows + 2 * width, width), :] = plane
            prim_v[f, pl.ds(rows + 3 * width, width), :] = plane

    for copy in quad_copies:
        copy.wait()

    def spread(slot, totals):
        index = ring_pos * (QUAD * 8) + slot
        live = slot % 8 < count_s[ring_pos * QUAD + slot // 8]
        code = jnp.where(live, owner_s[index] * 2 + block_s[index], -1)
        relative = code - 2 * quad_pos - lane_block
        value = quad_v[slot // 8, pl.ds(pl.multiple_of(slot % 8 * 8, 8), 8), :]
        return tuple(
            total + jnp.where(relative == 2 * QUAD * k, value, 0.0)
            for k, total in enumerate(totals)
        )

    totals = lax.fori_loop(
        0, QUAD * 8, spread, tuple(jnp.zeros((8, 128), F32) for _ in range(ring_n))
    )
    for k in range(ring_n):
        out_v[k] = totals[k]
    ring_copies = []
    for step in ring_steps:
        to = (ring_pos + step) % ring_n
        copy = remote(
            out_v.at[to], in_v.at[ring_pos], ring_send.at[step], ring_recv.at[step],
            to * QUAD + quad_pos, gz,
        )
        copy.start()
        ring_copies.append(copy)

    def sweep(load_plane, faces, normal, emit):
        before, cell = load_plane(0), load_plane(1)
        after = load_plane(2)
        diff = [b - a for a, b in zip(before, cell)]
        diff_up = [b - a for a, b in zip(cell, after)]
        left = [c + half_slope(a, b) for a, b, c in zip(diff, diff_up, cell)]

        def face(k, carry):
            cell, diff, left, flux_low = carry
            after = load_plane(k + 3)
            diff_up = [b - a for a, b in zip(cell, after)]
            slope = [half_slope(a, b) for a, b in zip(diff, diff_up)]
            right = [c - s for c, s in zip(cell, slope)]
            flux = double_flux(left, right, normal)
            return after, diff_up, [c + s for c, s in zip(cell, slope)], flux

        carry = face(0, (after, diff_up, left, None))

        def body(k, carry):
            low = carry[3]
            carry = face(k, carry)
            emit(k - 1, [b - a for a, b in zip(low, carry[3])])
            return carry

        lax.fori_loop(1, faces, body, carry)

    ahead.wait()
    back.wait()

    def theta_plane(k):
        return [cross_v[f, pl.ds(pl.multiple_of(k * depth, depth), depth), :] for f in range(8)]

    def theta_emit(k, change):
        for f in range(8):
            at = pl.ds(k, depth, stride=width)
            res_ref[f, at, :] = res_ref[f, at, :] - turn * change[f]

    sweep(theta_plane, width + 1, 1, theta_emit)

    @pl.when(not_first)
    def _():
        up.wait_recv()
        down.wait_send()

    @pl.when(not_last)
    def _():
        up.wait_send()
        down.wait_recv()

    for half in range(2):

        def axial_plane(k):
            at = pl.multiple_of(k * width + half * 8, 8)
            return [prim_v[f, pl.ds(at, 8), :] for f in range(8)]

        def axial_emit(k, change):
            at = pl.ds(pl.multiple_of(k * width + half * 8, 8), 8)
            for f in range(8):
                res_ref[f, at, :] = res_ref[f, at, :] - 0.5 * change[f]

        sweep(axial_plane, depth + 1, 2, axial_emit)

    across.wait()
    cell = [turned_v[f : f + 1, :] for f in range(8)]
    left = [
        cell[f]
        + half_slope(cell[f] - edge_in[f : f + 1, :], turned_v[8 + f : 9 + f, :])
        for f in range(8)
    ]
    face_one = double_flux(left, [turned_v[16 + f : 17 + f, :] for f in range(8)], 0)

    for copy in ring_copies:
        copy.wait()
    registers = out_v[ring_pos]
    for step in range(1, ring_n):
        registers = registers + in_v[(ring_pos + step) % ring_n]
    mismatch = registers - coarse
    inner = jnp.concatenate([0.5 * v for v in face_one], axis=0)
    for z in range(depth):
        shift = (128 - z * width) % 128
        at = pl.ds(z, 8, stride=depth)
        mis_ref[at, :] = (pltpu.roll(mismatch, shift, 1) if shift else mismatch)[:, :width]
        inner_ref[at, :] = (pltpu.roll(inner, shift, 1) if shift else inner)[:, :width]
    face = (BR * level).astype(F32)
    added = mismatch * (face / (face + 0.5))
    nothing = jnp.zeros((1, 128), F32)
    inner_part, outer_part = [], []
    for f in range(8):
        inner_part += [-face_one[f], face_one[f] * (1.0 / 3.0), nothing, nothing]
        outer_part += [added[f : f + 1], nothing, nothing, nothing]
    corr_v[...] = jnp.concatenate(inner_part + outer_part * 3, axis=0).T

    hits = [(lane < 2) | (lane == BR * depth_of[half]) for half in range(2)]

    def correct(z, _):
        for half in range(2):
            at = pl.ds(pl.multiple_of(z * width + half * 8, 8), 8)
            corr = corr_v[at, :]
            for f in range(8):
                moved = pltpu.roll(corr, 128 - 4 * f, 1) if f else corr
                res_ref[f, at, :] = res_ref[f, at, :] + jnp.where(hits[half], moved, 0.0)
        return 0

    lax.fori_loop(0, depth, correct, 0)


def copy_out(*refs):
    count = len(refs) // 2
    copies = [
        pltpu.make_async_copy(refs[i], refs[count + i], refs[-1].at[i]) for i in range(count)
    ]
    for copy in copies:
        copy.start()
    for copy in copies:
        copy.wait()


def body(mesh_shape, fluid_state, levels, fine_rim, slot_owner, slot_block, slot_count):
    fields, depth, width, radial = fluid_state.shape
    theta_n, gz_n = mesh_shape
    rows = depth * width
    ring_n = theta_n // QUAD
    slots = fine_rim.shape[0]
    sizes = (theta_n, gz_n, depth, width, 2.0 * math.pi / (width * theta_n))
    hbm = pl.BlockSpec(memory_space=pltpu.MemorySpace.HBM)
    vmem = pl.BlockSpec(memory_space=pltpu.MemorySpace.VMEM)
    res, mis, inner = pl.pallas_call(
        functools.partial(kernel, sizes),
        out_shape=(
            jax.ShapeDtypeStruct((fields, rows, radial), F32),
            jax.ShapeDtypeStruct((fields * depth, width), F32),
            jax.ShapeDtypeStruct((fields * depth, width), F32),
        ),
        in_specs=[hbm] * 6,
        out_specs=(vmem, vmem, vmem),
        scratch_shapes=[
            pltpu.VMEM((fields, rows, radial), F32),
            pltpu.VMEM((slots * 2 * fields, 128), F32),
            pltpu.VMEM((fields, rows + 4 * width, radial), F32),
            pltpu.VMEM((fields, rows + 4 * depth, radial), F32),
            pltpu.VMEM((8, 128), F32),
            pltpu.VMEM((8, 128), F32),
            pltpu.VMEM((rows, 128), F32),
            pltpu.VMEM((128, rows), F32),
            pltpu.VMEM((rows, 128), F32),
            pltpu.VMEM((QUAD, slots * fields, 128), F32),
            pltpu.VMEM((ring_n, 8, 128), F32),
            pltpu.VMEM((ring_n, 8, 128), F32),
            pltpu.SMEM((2, 4), jnp.int32),
            pltpu.SMEM(slot_owner.shape, jnp.int32),
            pltpu.SMEM(slot_block.shape, jnp.int32),
            pltpu.SMEM(slot_count.shape, jnp.int32),
            pltpu.SemaphoreType.DMA((6,)),
            pltpu.SemaphoreType.DMA((QUAD,)),
            pltpu.SemaphoreType.DMA((QUAD,)),
            pltpu.SemaphoreType.DMA((ring_n,)),
            pltpu.SemaphoreType.DMA((ring_n,)),
            pltpu.SemaphoreType.DMA((5,)),
            pltpu.SemaphoreType.DMA((5,)),
        ],
        compiler_params=pltpu.CompilerParams(
            collective_id=0, has_side_effects=True, vmem_limit_bytes=32 * 1024 * 1024
        ),
    )(
        *(
            pltpu.with_memory_space_constraint(v, pltpu.MemorySpace.HBM)
            for v in (
                fluid_state.reshape(fields, rows, radial),
                fine_rim.reshape(slots * 2 * fields, 128),
                levels.T,
                slot_owner,
                slot_block,
                slot_count,
            )
        )
    )
    outs = (res, mis, inner)
    res, mis, inner = pl.pallas_call(
        copy_out,
        out_shape=tuple(jax.ShapeDtypeStruct(v.shape, F32) for v in outs),
        in_specs=[vmem] * 3,
        out_specs=(hbm,) * 3,
        scratch_shapes=[pltpu.SemaphoreType.DMA((3,))],
        compiler_params=pltpu.CompilerParams(vmem_limit_bytes=2 * 1024 * 1024),
    )(*outs)
    return (
        res.reshape(fields, depth, width, radial),
        mis.reshape(fields, depth, width),
        inner.reshape(fields, depth, width),
    )


def solution(mesh):
    return jax.shard_map(
        functools.partial(body, (mesh.shape["theta"], mesh.shape["gz"])),
        mesh=mesh,
        in_specs=(
            P(None, "gz", "theta", None),
            P(None, "theta"),
            P("theta", None, None, "gz"),
            P(),
            P(),
            P(),
        ),
        out_specs=(P(None, "gz", "theta", None), P(None, "gz", "theta"), P(None, "gz", "theta")),
        check_vma=False,
    )
```

```python
import functools
import math

import jax
import jax.numpy as jnp
from jax import lax
from jax.experimental import pallas as pl
from jax.experimental.pallas import tpu as pltpu
from jax.sharding import PartitionSpec as P

BT = 8
BR = 32
GAMMA = 5.0 / 3.0
QUAD = 4
F32 = jnp.float32
MESH = pl.DeviceIdType.MESH


def primitive(cons):
    rho, mr, mt, mz, energy, br, bt, bz = cons
    inv = 1.0 / rho
    vr, vt, vz = mr * inv, mt * inv, mz * inv
    kinetic = mr * vr + mt * vt + mz * vz
    magnetic = br * br + bt * bt + bz * bz
    pressure = (GAMMA - 1.0) * (energy - 0.5 * (kinetic + magnetic))
    return [rho, vr, vt, vz, pressure, br, bt, bz]


def side_state(state, normal):
    rho, pressure = state[0], state[4]
    vel, field = state[1:4], state[5:8]
    mom = [rho * v for v in vel]
    vel_n, field_n = vel[normal], field[normal]
    field_sq = field[0] * field[0] + field[1] * field[1] + field[2] * field[2]
    half_sq = 0.5 * field_sq
    kinetic = 0.5 * (mom[0] * vel[0] + mom[1] * vel[1] + mom[2] * vel[2])
    vel_dot = vel[0] * field[0] + vel[1] * field[1] + vel[2] * field[2]
    total_p = pressure + half_sq
    energy = pressure * (1.0 / (GAMMA - 1.0)) + kinetic + half_sq
    flux = [mom[normal]]
    for comp in range(3):
        term = mom[comp] * vel_n - field[comp] * field_n
        flux.append(term + total_p if comp == normal else term)
    flux.append((energy + total_p) * vel_n - field_n * vel_dot)
    for comp in range(3):
        flux.append(None if comp == normal else vel_n * field[comp] - field_n * vel[comp])
    fast = GAMMA * pressure + field_sq
    signal = jnp.abs(vel_n) + fast * lax.rsqrt(fast * rho)
    return [rho] + mom + [energy] + list(field), flux, signal


def double_flux(left, right, normal):
    cons_l, flux_l, signal_l = side_state(left, normal)
    cons_r, flux_r, signal_r = side_state(right, normal)
    top = jnp.maximum(signal_l, signal_r)
    out = []
    for ul, ur, fl, fr in zip(cons_l, cons_r, flux_l, flux_r):
        if fl is None:
            out.append(top * (ul - ur))
        else:
            out.append((fl + fr) - top * (ur - ul))
    return out


def half_slope(lower, upper):
    low, high = jnp.minimum(lower, upper), jnp.maximum(lower, upper)
    return 0.5 * (jnp.maximum(low, 0.0) + jnp.minimum(high, 0.0))


def kernel(
    sizes,
    x_hbm, fine_hbm, levels_hbm, owner_hbm, block_hbm, count_hbm,
    res_ref, mis_ref, inner_ref,
    x_v, fine_v, prim_v, cross_v, edge_v, edge_in, packed_v, turned_v, corr_v,
    quad_v, out_v, in_v,
    levels_s, owner_s, block_s, count_s,
    load_sem, quad_send, quad_recv, ring_send, ring_recv, halo_send, halo_recv, news_sem,
):
    theta_n, gz_n, depth, width, dtheta = sizes
    rows = depth * width
    ring_n = theta_n // QUAD
    theta = lax.axis_index("theta")
    gz = lax.axis_index("gz")
    ring_pos, quad_pos = theta // QUAD, theta % QUAD

    def load(src, dst, sem):
        return pltpu.make_async_copy(src, dst, load_sem.at[sem])

    loads = [
        load(fine_hbm, fine_v, 0),
        load(x_hbm, x_v, 1),
        load(levels_hbm, levels_s, 2),
        load(owner_hbm, owner_s, 3),
        load(block_hbm, block_s, 4),
        load(count_hbm, count_s, 5),
    ]
    for item in loads:
        item.start()

    barrier = pltpu.get_barrier_semaphore()
    half_n = ring_n // 2
    early = ring_pos < half_n
    half_at = ring_pos // half_n * half_n

    def signal(sem, t, g):
        pl.semaphore_signal(sem, inc=1, device_id={"theta": t, "gz": g}, device_id_type=MESH)

    def same_ring(step):
        return half_at + (ring_pos - half_at + step) % half_n

    def other_ring(step):
        return half_n - half_at + (ring_pos - half_at + step) % half_n

    def hear(role, count):
        @pl.when(quad_pos == role)
        def _():
            pl.semaphore_wait(barrier, count)
            for step in range(1, QUAD):
                signal(news_sem.at[role], ring_pos * QUAD + (role + step) % QUAD, gz)

    def heed(role):
        @pl.when(quad_pos != role)
        def _():
            pl.semaphore_wait(news_sem.at[role], 1)

    @pl.when(quad_pos != 0)
    def _():
        signal(barrier, ring_pos * QUAD, gz)

    lane = lax.broadcasted_iota(jnp.int32, (8, 128), 1)
    lane_block = (lane % width) // BT

    loads[0].wait()
    sides = [
        [fine_v[pl.ds(side * 8 + var, 8, stride=16), :] for var in range(8)] for side in (0, 1)
    ]
    fine_flux = jnp.concatenate(double_flux(sides[0], sides[1], 0), axis=0)
    src = lax.broadcasted_iota(jnp.int32, (128, 128), 0)
    dst = lax.broadcasted_iota(jnp.int32, (128, 128), 1)
    pairing = jnp.where(
        (src // width == dst // width) & ((src % width) // 2 == dst % BT), 0.125, 0.0
    ).astype(F32)
    partial = jnp.dot(
        fine_flux, pairing, precision=lax.Precision.HIGHEST, preferred_element_type=F32
    )
    for var in range(8):
        quad_v[quad_pos, pl.ds(var, 8, stride=8), :] = partial[var * 8 : var * 8 + 8]

    hear(0, QUAD - 1)

    loads[1].wait()

    def to_primitive(z, _):
        at = pl.multiple_of(z * width, width)
        for half in range(2):
            prims = primitive([x_v[f, pl.ds(at + half * 8, 8), :] for f in range(8)])
            for f, value in enumerate(prims):
                prim_v[f, pl.ds(at + 2 * width + half * 8, 8), :] = value
                cross_v[f, pl.ds((2 + half * 8) * depth + z, 8, stride=depth), :] = value
        return 0

    lax.fori_loop(0, depth, to_primitive, 0)

    for item in loads[2:]:
        item.wait()
    heed(0)

    @pl.when(quad_pos == 1)
    def _():
        for step in range(1, half_n):
            signal(barrier, same_ring(step) * QUAD + 1, gz)

    @pl.when(quad_pos == 2)
    def _():
        for step in range(half_n):
            signal(barrier, other_ring(step) * QUAD + 2, gz)

    @pl.when(quad_pos == 3)
    def _():
        for t, g in (
            ((theta + QUAD) % theta_n, gz),
            ((theta + theta_n - QUAD) % theta_n, gz),
            (theta, (gz + 1) % gz_n),
            (theta, (gz + gz_n - 1) % gz_n),
        ):
            signal(barrier, t, g)

    def remote(src, dst, send, recv, t, g):
        return pltpu.make_async_remote_copy(
            src_ref=src, dst_ref=dst, send_sem=send, recv_sem=recv,
            device_id={"theta": t, "gz": g}, device_id_type=MESH,
        )

    quad_copies = []
    for step in range(1, QUAD):
        copy = remote(
            quad_v.at[quad_pos], quad_v.at[quad_pos], quad_send.at[step], quad_recv.at[step],
            ring_pos * QUAD + (quad_pos + step) % QUAD, gz,
        )
        copy.start()
        quad_copies.append(copy)

    radius = lane.astype(F32) + 0.5
    inv_radius = 1.0 / radius
    inward = jnp.where(lane == 1, 0.0, 0.5 * (radius - 0.5) * inv_radius)
    outward = jnp.where(lane == 0, 0.0, 0.5 * (radius + 0.5) * inv_radius)
    turn = inv_radius * (0.5 / dtheta)
    last = lane == 127
    spot = jnp.where(lane >= BR, lane % BR, -1)

    def radial(z, _):
        for half in range(2):
            at = pl.multiple_of(z * width + half * 8, 8)
            left, right = [], []
            cell = [prim_v[f, pl.ds(at + 2 * width, 8), :] for f in range(8)]
            packed = jnp.zeros((8, 128), F32)
            for f in range(8):
                mid = cell[f]
                lower = mid - pltpu.roll(mid, 1, 1)
                upper = jnp.where(last, 0.0, pltpu.roll(lower, 127, 1))
                slope = half_slope(lower, upper)
                left.append(mid + slope)
                right.append(jnp.where(last, mid, pltpu.roll(mid - slope, 127, 1)))
                packed = jnp.where(lane == f, pltpu.roll(mid, f, 1) if f else mid, packed)
                packed = jnp.where(lane == f + 8, pltpu.roll(upper, f + 8, 1), packed)
                packed = jnp.where(lane == f + 16, pltpu.roll(right[f], f + 16, 1), packed)
            flux = double_flux(left, right, 0)
            rho, vr, vt, _, pressure, br, bt, bz = cell
            out = [inward * pltpu.roll(v, 1, 1) - outward * v for v in flux]
            field_sq = br * br + bt * bt + bz * bz
            out[1] = out[1] + inv_radius * (rho * vt * vt + pressure + 0.5 * field_sq - bt * bt)
            out[2] = out[2] - inv_radius * (rho * vr * vt - br * bt)
            out[6] = out[6] + inv_radius * (vr * bt - vt * br)
            for f in range(8):
                res_ref[f, pl.ds(at, 8), :] = out[f]
                packed = jnp.where(spot == f, pltpu.roll(flux[f], f + 1, 1), packed)
            packed_v[pl.ds(at, 8), :] = packed
        return 0

    lax.fori_loop(0, depth, radial, 0)
    turned_v[...] = packed_v[...].T
    row = lax.broadcasted_iota(jnp.int32, (8, 128), 0)
    flip = (row == 1) | (row == 2) | (row == 5) | (row == 6)
    edge_v[...] = jnp.where(flip, -turned_v[0:8, :], turned_v[0:8, :])

    depth_of = [levels_s[b, 0] + levels_s[b, 1] + levels_s[b, 2] + levels_s[b, 3] for b in range(2)]
    level = jnp.where(lane_block == 0, depth_of[0], depth_of[1])
    coarse = 0.5 * jnp.where(
        level == 1,
        turned_v[BR : BR + 8, :],
        jnp.where(level == 2, turned_v[2 * BR : 2 * BR + 8, :], turned_v[3 * BR : 3 * BR + 8, :]),
    )

    across = remote(
        edge_v, edge_in, halo_send.at[0], halo_recv.at[0], (theta + theta_n // 2) % theta_n, gz
    )
    two_z, two_t = 2 * width, 2 * depth
    up = remote(
        prim_v.at[:, pl.ds(rows, two_z)], prim_v.at[:, pl.ds(0, two_z)],
        halo_send.at[1], halo_recv.at[1], theta, (gz + 1) % gz_n,
    )
    down = remote(
        prim_v.at[:, pl.ds(two_z, two_z)], prim_v.at[:, pl.ds(rows + two_z, two_z)],
        halo_send.at[2], halo_recv.at[2], theta, (gz + gz_n - 1) % gz_n,
    )
    not_last, not_first = gz < gz_n - 1, gz > 0
    ahead = remote(
        cross_v.at[:, pl.ds(rows, two_t)], cross_v.at[:, pl.ds(0, two_t)],
        halo_send.at[3], halo_recv.at[3], (theta + 1) % theta_n, gz,
    )
    back = remote(
        cross_v.at[:, pl.ds(two_t, two_t)], cross_v.at[:, pl.ds(rows + two_t, two_t)],
        halo_send.at[4], halo_recv.at[4], (theta + theta_n - 1) % theta_n, gz,
    )

    def send_halos():
        ahead.start()
        back.start()
        pl.when(not_last)(up.start)
        pl.when(not_first)(down.start)

    @pl.when(gz == 0)
    def _():
        for f in range(8):
            plane = prim_v[f, pl.ds(two_z, width), :]
            prim_v[f, pl.ds(0, width), :] = plane
            prim_v[f, pl.ds(width, width), :] = plane

    @pl.when(gz == gz_n - 1)
    def _():
        for f in range(8):
            plane = prim_v[f, pl.ds(rows + width, width), :]
            prim_v[f, pl.ds(rows + 2 * width, width), :] = plane
            prim_v[f, pl.ds(rows + 3 * width, width), :] = plane

    hear(3, 4)
    heed(3)

    for copy in quad_copies:
        copy.wait()

    def spread(slot, totals):
        index = ring_pos * (QUAD * 8) + slot
        live = slot % 8 < count_s[ring_pos * QUAD + slot // 8]
        code = jnp.where(live, owner_s[index] * 2 + block_s[index], -1)
        relative = code - 2 * quad_pos - lane_block
        value = quad_v[slot // 8, pl.ds(pl.multiple_of(slot % 8 * 8, 8), 8), :]
        return tuple(
            total + jnp.where(relative == 2 * QUAD * k, value, 0.0)
            for k, total in enumerate(totals)
        )

    totals = lax.fori_loop(
        0, QUAD * 8, spread, tuple(jnp.zeros((8, 128), F32) for _ in range(ring_n))
    )
    for k in range(ring_n):
        out_v[k] = totals[k]

    def ring_copy(to, slot):
        return remote(
            out_v.at[to], in_v.at[ring_pos], ring_send.at[slot], ring_recv.at[slot],
            to * QUAD + quad_pos, gz,
        )

    same_copies = [ring_copy(same_ring(step), step) for step in range(1, half_n)]
    other_copies = [ring_copy(other_ring(step), half_n + step) for step in range(half_n)]

    def send_same():
        hear(1, half_n - 1)
        heed(1)
        for copy in same_copies:
            copy.start()

    @pl.when(early)
    def _():
        send_halos()
        send_same()

    hear(2, half_n)
    heed(2)
    for copy in other_copies:
        copy.start()
    across.start()

    @pl.when(jnp.logical_not(early))
    def _():
        send_halos()
        send_same()

    ring_copies = same_copies + other_copies

    def sweep(load_plane, faces, normal, emit):
        before, cell = load_plane(0), load_plane(1)
        after = load_plane(2)
        diff = [b - a for a, b in zip(before, cell)]
        diff_up = [b - a for a, b in zip(cell, after)]
        left = [c + half_slope(a, b) for a, b, c in zip(diff, diff_up, cell)]

        def face(k, carry):
            cell, diff, left, flux_low = carry
            after = load_plane(k + 3)
            diff_up = [b - a for a, b in zip(cell, after)]
            slope = [half_slope(a, b) for a, b in zip(diff, diff_up)]
            right = [c - s for c, s in zip(cell, slope)]
            flux = double_flux(left, right, normal)
            return after, diff_up, [c + s for c, s in zip(cell, slope)], flux

        carry = face(0, (after, diff_up, left, None))

        def body(k, carry):
            low = carry[3]
            carry = face(k, carry)
            emit(k - 1, [b - a for a, b in zip(low, carry[3])])
            return carry

        lax.fori_loop(1, faces, body, carry)

    ahead.wait()
    back.wait()

    def theta_plane(k):
        return [cross_v[f, pl.ds(pl.multiple_of(k * depth, depth), depth), :] for f in range(8)]

    def theta_emit(k, change):
        for f in range(8):
            at = pl.ds(k, depth, stride=width)
            res_ref[f, at, :] = res_ref[f, at, :] - turn * change[f]

    sweep(theta_plane, width + 1, 1, theta_emit)

    @pl.when(not_first)
    def _():
        up.wait_recv()
        down.wait_send()

    @pl.when(not_last)
    def _():
        up.wait_send()
        down.wait_recv()

    for half in range(2):

        def axial_plane(k):
            at = pl.multiple_of(k * width + half * 8, 8)
            return [prim_v[f, pl.ds(at, 8), :] for f in range(8)]

        def axial_emit(k, change):
            at = pl.ds(pl.multiple_of(k * width + half * 8, 8), 8)
            for f in range(8):
                res_ref[f, at, :] = res_ref[f, at, :] - 0.5 * change[f]

        sweep(axial_plane, depth + 1, 2, axial_emit)

    across.wait()
    cell = [turned_v[f : f + 1, :] for f in range(8)]
    left = [
        cell[f]
        + half_slope(cell[f] - edge_in[f : f + 1, :], turned_v[8 + f : 9 + f, :])
        for f in range(8)
    ]
    face_one = double_flux(left, [turned_v[16 + f : 17 + f, :] for f in range(8)], 0)

    for copy in ring_copies:
        copy.wait()
    registers = out_v[ring_pos]
    for step in range(1, ring_n):
        registers = registers + in_v[(ring_pos + step) % ring_n]
    mismatch = registers - coarse
    inner = jnp.concatenate([0.5 * v for v in face_one], axis=0)
    for z in range(depth):
        shift = (128 - z * width) % 128
        at = pl.ds(z, 8, stride=depth)
        mis_ref[at, :] = (pltpu.roll(mismatch, shift, 1) if shift else mismatch)[:, :width]
        inner_ref[at, :] = (pltpu.roll(inner, shift, 1) if shift else inner)[:, :width]
    face = (BR * level).astype(F32)
    added = mismatch * (face / (face + 0.5))
    nothing = jnp.zeros((1, 128), F32)
    inner_part, outer_part = [], []
    for f in range(8):
        inner_part += [-face_one[f], face_one[f] * (1.0 / 3.0), nothing, nothing]
        outer_part += [added[f : f + 1], nothing, nothing, nothing]
    corr_v[...] = jnp.concatenate(inner_part + outer_part * 3, axis=0).T

    hits = [(lane < 2) | (lane == BR * depth_of[half]) for half in range(2)]

    def correct(z, _):
        for half in range(2):
            at = pl.ds(pl.multiple_of(z * width + half * 8, 8), 8)
            corr = corr_v[at, :]
            for f in range(8):
                moved = pltpu.roll(corr, 128 - 4 * f, 1) if f else corr
                res_ref[f, at, :] = res_ref[f, at, :] + jnp.where(hits[half], moved, 0.0)
        return 0

    lax.fori_loop(0, depth, correct, 0)


def copy_out(*refs):
    count = len(refs) // 2
    copies = [
        pltpu.make_async_copy(refs[i], refs[count + i], refs[-1].at[i]) for i in range(count)
    ]
    for copy in copies:
        copy.start()
    for copy in copies:
        copy.wait()


def body(mesh_shape, fluid_state, levels, fine_rim, slot_owner, slot_block, slot_count):
    fields, depth, width, radial = fluid_state.shape
    theta_n, gz_n = mesh_shape
    rows = depth * width
    ring_n = theta_n // QUAD
    slots = fine_rim.shape[0]
    sizes = (theta_n, gz_n, depth, width, 2.0 * math.pi / (width * theta_n))
    hbm = pl.BlockSpec(memory_space=pltpu.MemorySpace.HBM)
    vmem = pl.BlockSpec(memory_space=pltpu.MemorySpace.VMEM)
    res, mis, inner = pl.pallas_call(
        functools.partial(kernel, sizes),
        out_shape=(
            jax.ShapeDtypeStruct((fields, rows, radial), F32),
            jax.ShapeDtypeStruct((fields * depth, width), F32),
            jax.ShapeDtypeStruct((fields * depth, width), F32),
        ),
        in_specs=[hbm] * 6,
        out_specs=(vmem, vmem, vmem),
        scratch_shapes=[
            pltpu.VMEM((fields, rows, radial), F32),
            pltpu.VMEM((slots * 2 * fields, 128), F32),
            pltpu.VMEM((fields, rows + 4 * width, radial), F32),
            pltpu.VMEM((fields, rows + 4 * depth, radial), F32),
            pltpu.VMEM((8, 128), F32),
            pltpu.VMEM((8, 128), F32),
            pltpu.VMEM((rows, 128), F32),
            pltpu.VMEM((128, rows), F32),
            pltpu.VMEM((rows, 128), F32),
            pltpu.VMEM((QUAD, slots * fields, 128), F32),
            pltpu.VMEM((ring_n, 8, 128), F32),
            pltpu.VMEM((ring_n, 8, 128), F32),
            pltpu.SMEM((2, 4), jnp.int32),
            pltpu.SMEM(slot_owner.shape, jnp.int32),
            pltpu.SMEM(slot_block.shape, jnp.int32),
            pltpu.SMEM(slot_count.shape, jnp.int32),
            pltpu.SemaphoreType.DMA((6,)),
            pltpu.SemaphoreType.DMA((QUAD,)),
            pltpu.SemaphoreType.DMA((QUAD,)),
            pltpu.SemaphoreType.DMA((ring_n,)),
            pltpu.SemaphoreType.DMA((ring_n,)),
            pltpu.SemaphoreType.DMA((5,)),
            pltpu.SemaphoreType.DMA((5,)),
            pltpu.SemaphoreType.REGULAR((4,)),
        ],
        compiler_params=pltpu.CompilerParams(
            collective_id=0, has_side_effects=True, vmem_limit_bytes=32 * 1024 * 1024
        ),
    )(
        *(
            pltpu.with_memory_space_constraint(v, pltpu.MemorySpace.HBM)
            for v in (
                fluid_state.reshape(fields, rows, radial),
                fine_rim.reshape(slots * 2 * fields, 128),
                levels.T,
                slot_owner,
                slot_block,
                slot_count,
            )
        )
    )
    outs = (res, mis, inner)
    res, mis, inner = pl.pallas_call(
        copy_out,
        out_shape=tuple(jax.ShapeDtypeStruct(v.shape, F32) for v in outs),
        in_specs=[vmem] * 3,
        out_specs=(hbm,) * 3,
        scratch_shapes=[pltpu.SemaphoreType.DMA((3,))],
        compiler_params=pltpu.CompilerParams(vmem_limit_bytes=2 * 1024 * 1024),
    )(*outs)
    return (
        res.reshape(fields, depth, width, radial),
        mis.reshape(fields, depth, width),
        inner.reshape(fields, depth, width),
    )


def solution(mesh):
    return jax.shard_map(
        functools.partial(body, (mesh.shape["theta"], mesh.shape["gz"])),
        mesh=mesh,
        in_specs=(
            P(None, "gz", "theta", None),
            P(None, "theta"),
            P("theta", None, None, "gz"),
            P(),
            P(),
            P(),
        ),
        out_specs=(P(None, "gz", "theta", None), P(None, "gz", "theta"), P(None, "gz", "theta")),
        check_vma=False,
    )
```

```python
import functools
import math

import jax
import jax.numpy as jnp
from jax import lax
from jax.experimental import pallas as pl
from jax.experimental.pallas import tpu as pltpu
from jax.sharding import PartitionSpec as P

BT = 8
BR = 32
GAMMA = 5.0 / 3.0
QUAD = 4
F32 = jnp.float32
MESH = pl.DeviceIdType.MESH


def primitive(cons):
    rho, mr, mt, mz, energy, br, bt, bz = cons
    inv = 1.0 / rho
    vr, vt, vz = mr * inv, mt * inv, mz * inv
    kinetic = mr * vr + mt * vt + mz * vz
    magnetic = br * br + bt * bt + bz * bz
    pressure = (GAMMA - 1.0) * (energy - 0.5 * (kinetic + magnetic))
    return [rho, vr, vt, vz, pressure, br, bt, bz]


def side_state(state, normal):
    rho, pressure = state[0], state[4]
    vel, field = state[1:4], state[5:8]
    mom = [rho * v for v in vel]
    vel_n, field_n = vel[normal], field[normal]
    field_sq = field[0] * field[0] + field[1] * field[1] + field[2] * field[2]
    half_sq = 0.5 * field_sq
    kinetic = 0.5 * (mom[0] * vel[0] + mom[1] * vel[1] + mom[2] * vel[2])
    vel_dot = vel[0] * field[0] + vel[1] * field[1] + vel[2] * field[2]
    total_p = pressure + half_sq
    energy = pressure * (1.0 / (GAMMA - 1.0)) + kinetic + half_sq
    flux = [mom[normal]]
    for comp in range(3):
        term = mom[comp] * vel_n - field[comp] * field_n
        flux.append(term + total_p if comp == normal else term)
    flux.append((energy + total_p) * vel_n - field_n * vel_dot)
    for comp in range(3):
        flux.append(None if comp == normal else vel_n * field[comp] - field_n * vel[comp])
    fast = GAMMA * pressure + field_sq
    signal = jnp.abs(vel_n) + fast * lax.rsqrt(fast * rho)
    return [rho] + mom + [energy] + list(field), flux, signal


def double_flux(left, right, normal):
    cons_l, flux_l, signal_l = side_state(left, normal)
    cons_r, flux_r, signal_r = side_state(right, normal)
    top = jnp.maximum(signal_l, signal_r)
    out = []
    for ul, ur, fl, fr in zip(cons_l, cons_r, flux_l, flux_r):
        if fl is None:
            out.append(top * (ul - ur))
        else:
            out.append((fl + fr) - top * (ur - ul))
    return out


def half_slope(lower, upper):
    low, high = jnp.minimum(lower, upper), jnp.maximum(lower, upper)
    return 0.5 * (jnp.maximum(low, 0.0) + jnp.minimum(high, 0.0))


def kernel(
    sizes,
    x_hbm, fine_hbm, levels_hbm, owner_hbm, block_hbm, count_hbm,
    res_ref, mis_ref, inner_ref,
    x_v, fine_v, prim_v, cross_v, edge_v, edge_in, packed_v, turned_v, corr_v,
    quad_v, out_v, in_v,
    levels_s, owner_s, block_s, count_s,
    load_sem, quad_send, quad_recv, ring_send, ring_recv, halo_send, halo_recv, news_sem,
):
    theta_n, gz_n, depth, width, dtheta = sizes
    rows = depth * width
    ring_n = theta_n // QUAD
    theta = lax.axis_index("theta")
    gz = lax.axis_index("gz")
    ring_pos, quad_pos = theta // QUAD, theta % QUAD

    def load(src, dst, sem):
        return pltpu.make_async_copy(src, dst, load_sem.at[sem])

    loads = [
        load(fine_hbm, fine_v, 0),
        load(x_hbm, x_v, 1),
        load(levels_hbm, levels_s, 2),
        load(owner_hbm, owner_s, 3),
        load(block_hbm, block_s, 4),
        load(count_hbm, count_s, 5),
    ]
    for item in loads:
        item.start()

    barrier = pltpu.get_barrier_semaphore()
    half_n = ring_n // 2
    early = ring_pos < half_n
    late = jnp.logical_not(early)
    half_at = ring_pos // half_n * half_n
    core_zero = quad_pos % 2 == 0
    not_start, not_end = ring_pos > half_at, ring_pos < half_at + half_n - 1
    ring_near = not_start.astype(jnp.int32) + not_end.astype(jnp.int32)

    def signal(sem, t, g):
        pl.semaphore_signal(sem, inc=1, device_id={"theta": t, "gz": g}, device_id_type=MESH)

    def same_ring(step):
        return half_at + (ring_pos - half_at + step) % half_n

    def other_ring(step):
        return half_n - half_at + (ring_pos - half_at + step) % half_n

    def hear(role, count):
        @pl.when(quad_pos == role)
        def _():
            pl.semaphore_wait(barrier, count)
            for step in range(1, QUAD):
                signal(news_sem.at[role], ring_pos * QUAD + (role + step) % QUAD, gz)

    def heed(role):
        @pl.when(quad_pos != role)
        def _():
            pl.semaphore_wait(news_sem.at[role], 1)

    @pl.when(quad_pos != 0)
    def _():
        signal(barrier, ring_pos * QUAD, gz)

    @pl.when(late & (quad_pos != 2))
    def _():
        signal(barrier, ring_pos * QUAD + 2, gz)

    lane = lax.broadcasted_iota(jnp.int32, (8, 128), 1)
    lane_block = (lane % width) // BT

    loads[0].wait()
    sides = [
        [fine_v[pl.ds(side * 8 + var, 8, stride=16), :] for var in range(8)] for side in (0, 1)
    ]
    fine_flux = jnp.concatenate(double_flux(sides[0], sides[1], 0), axis=0)
    src = lax.broadcasted_iota(jnp.int32, (128, 128), 0)
    dst = lax.broadcasted_iota(jnp.int32, (128, 128), 1)
    pairing = jnp.where(
        (src // width == dst // width) & ((src % width) // 2 == dst % BT), 0.125, 0.0
    ).astype(F32)
    partial = jnp.dot(
        fine_flux, pairing, precision=lax.Precision.HIGHEST, preferred_element_type=F32
    )
    for var in range(8):
        quad_v[quad_pos, pl.ds(var, 8, stride=8), :] = partial[var * 8 : var * 8 + 8]

    pl.when(early)(functools.partial(hear, 0, QUAD - 1))

    @pl.when(late & core_zero)
    def _():
        pl.semaphore_wait(barrier, QUAD - 1)
        signal(news_sem.at[0], theta + 1, gz)

    loads[1].wait()

    def to_primitive(z, _):
        at = pl.multiple_of(z * width, width)
        for half in range(2):
            prims = primitive([x_v[f, pl.ds(at + half * 8, 8), :] for f in range(8)])
            for f, value in enumerate(prims):
                prim_v[f, pl.ds(at + 2 * width + half * 8, 8), :] = value
                cross_v[f, pl.ds((2 + half * 8) * depth + z, 8, stride=depth), :] = value
        return 0

    lax.fori_loop(0, depth, to_primitive, 0)

    for item in loads[2:]:
        item.wait()

    @pl.when((early & (quad_pos != 0)) | (late & jnp.logical_not(core_zero)))
    def _():
        pl.semaphore_wait(news_sem.at[0], 1)

    def remote(src, dst, send, recv, t, g):
        return pltpu.make_async_remote_copy(
            src_ref=src, dst_ref=dst, send_sem=send, recv_sem=recv,
            device_id={"theta": t, "gz": g}, device_id_type=MESH,
        )

    quad_copies = []
    for step in range(1, QUAD):
        copy = remote(
            quad_v.at[quad_pos], quad_v.at[quad_pos], quad_send.at[step], quad_recv.at[step],
            ring_pos * QUAD + (quad_pos + step) % QUAD, gz,
        )
        copy.start()
        quad_copies.append(copy)

    gz_next, gz_back = (gz + 1) % gz_n, (gz + gz_n - 1) % gz_n

    def greet_near():
        signal(barrier, theta, gz_next)
        signal(barrier, theta, gz_back)
        pl.when(not_start)(functools.partial(signal, barrier, theta - QUAD, gz))
        pl.when(not_end)(functools.partial(signal, barrier, theta + QUAD, gz))

    @pl.when(quad_pos == 1)
    def _():
        for step in range(half_n):
            signal(barrier, other_ring(step) * QUAD + 1, gz)
        pl.when(late)(greet_near)

    pl.when(early & (quad_pos == 2))(greet_near)

    @pl.when(quad_pos == 3)
    def _():
        for step in range(1, half_n):
            signal(barrier, same_ring(step) * QUAD + 3, gz)

    radius = lane.astype(F32) + 0.5
    inv_radius = 1.0 / radius
    inward = jnp.where(lane == 1, 0.0, 0.5 * (radius - 0.5) * inv_radius)
    outward = jnp.where(lane == 0, 0.0, 0.5 * (radius + 0.5) * inv_radius)
    turn = inv_radius * (0.5 / dtheta)
    last = lane == 127
    spot = jnp.where(lane >= BR, lane % BR, -1)

    def radial(z, _):
        for half in range(2):
            at = pl.multiple_of(z * width + half * 8, 8)
            left, right = [], []
            cell = [prim_v[f, pl.ds(at + 2 * width, 8), :] for f in range(8)]
            packed = jnp.zeros((8, 128), F32)
            for f in range(8):
                mid = cell[f]
                lower = mid - pltpu.roll(mid, 1, 1)
                upper = jnp.where(last, 0.0, pltpu.roll(lower, 127, 1))
                slope = half_slope(lower, upper)
                left.append(mid + slope)
                right.append(jnp.where(last, mid, pltpu.roll(mid - slope, 127, 1)))
                packed = jnp.where(lane == f, pltpu.roll(mid, f, 1) if f else mid, packed)
                packed = jnp.where(lane == f + 8, pltpu.roll(upper, f + 8, 1), packed)
                packed = jnp.where(lane == f + 16, pltpu.roll(right[f], f + 16, 1), packed)
            flux = double_flux(left, right, 0)
            rho, vr, vt, _, pressure, br, bt, bz = cell
            out = [inward * pltpu.roll(v, 1, 1) - outward * v for v in flux]
            field_sq = br * br + bt * bt + bz * bz
            out[1] = out[1] + inv_radius * (rho * vt * vt + pressure + 0.5 * field_sq - bt * bt)
            out[2] = out[2] - inv_radius * (rho * vr * vt - br * bt)
            out[6] = out[6] + inv_radius * (vr * bt - vt * br)
            for f in range(8):
                res_ref[f, pl.ds(at, 8), :] = out[f]
                packed = jnp.where(spot == f, pltpu.roll(flux[f], f + 1, 1), packed)
            packed_v[pl.ds(at, 8), :] = packed
        return 0

    lax.fori_loop(0, depth, radial, 0)
    turned_v[...] = packed_v[...].T
    row = lax.broadcasted_iota(jnp.int32, (8, 128), 0)
    flip = (row == 1) | (row == 2) | (row == 5) | (row == 6)
    edge_v[...] = jnp.where(flip, -turned_v[0:8, :], turned_v[0:8, :])

    depth_of = [levels_s[b, 0] + levels_s[b, 1] + levels_s[b, 2] + levels_s[b, 3] for b in range(2)]
    level = jnp.where(lane_block == 0, depth_of[0], depth_of[1])
    coarse = 0.5 * jnp.where(
        level == 1,
        turned_v[BR : BR + 8, :],
        jnp.where(level == 2, turned_v[2 * BR : 2 * BR + 8, :], turned_v[3 * BR : 3 * BR + 8, :]),
    )

    across = remote(
        edge_v, edge_in, halo_send.at[0], halo_recv.at[0], (theta + theta_n // 2) % theta_n, gz
    )
    two_z, two_t = 2 * width, 2 * depth
    up = remote(
        prim_v.at[:, pl.ds(rows, two_z)], prim_v.at[:, pl.ds(0, two_z)],
        halo_send.at[1], halo_recv.at[1], theta, (gz + 1) % gz_n,
    )
    down = remote(
        prim_v.at[:, pl.ds(two_z, two_z)], prim_v.at[:, pl.ds(rows + two_z, two_z)],
        halo_send.at[2], halo_recv.at[2], theta, (gz + gz_n - 1) % gz_n,
    )
    not_last, not_first = gz < gz_n - 1, gz > 0
    ahead = remote(
        cross_v.at[:, pl.ds(rows, two_t)], cross_v.at[:, pl.ds(0, two_t)],
        halo_send.at[3], halo_recv.at[3], (theta + 1) % theta_n, gz,
    )
    back = remote(
        cross_v.at[:, pl.ds(two_t, two_t)], cross_v.at[:, pl.ds(rows + two_t, two_t)],
        halo_send.at[4], halo_recv.at[4], (theta + theta_n - 1) % theta_n, gz,
    )

    ahead_waits = theta == theta_n // 2 - 1
    back_waits = theta == 0

    def send_halos():
        pl.when(jnp.logical_not(ahead_waits))(ahead.start)
        pl.when(jnp.logical_not(back_waits))(back.start)
        pl.when(not_last)(up.start)
        pl.when(not_first)(down.start)

    @pl.when(gz == 0)
    def _():
        for f in range(8):
            plane = prim_v[f, pl.ds(two_z, width), :]
            prim_v[f, pl.ds(0, width), :] = plane
            prim_v[f, pl.ds(width, width), :] = plane

    @pl.when(gz == gz_n - 1)
    def _():
        for f in range(8):
            plane = prim_v[f, pl.ds(rows + width, width), :]
            prim_v[f, pl.ds(rows + 2 * width, width), :] = plane
            prim_v[f, pl.ds(rows + 3 * width, width), :] = plane

    @pl.when(early)
    def _():
        hear(2, 2 + ring_near)
        heed(2)
        send_halos()

    pl.when(late)(functools.partial(hear, 1, half_n + 2 + ring_near))

    for copy in quad_copies:
        copy.wait()

    def spread(slot, totals):
        index = ring_pos * (QUAD * 8) + slot
        live = slot % 8 < count_s[ring_pos * QUAD + slot // 8]
        code = jnp.where(live, owner_s[index] * 2 + block_s[index], -1)
        relative = code - 2 * quad_pos - lane_block
        value = quad_v[slot // 8, pl.ds(pl.multiple_of(slot % 8 * 8, 8), 8), :]
        return tuple(
            total + jnp.where(relative == 2 * QUAD * k, value, 0.0)
            for k, total in enumerate(totals)
        )

    totals = lax.fori_loop(
        0, QUAD * 8, spread, tuple(jnp.zeros((8, 128), F32) for _ in range(ring_n))
    )
    for k in range(ring_n):
        out_v[k] = totals[k]

    def ring_copy(to, slot):
        return remote(
            out_v.at[to], in_v.at[ring_pos], ring_send.at[slot], ring_recv.at[slot],
            to * QUAD + quad_pos, gz,
        )

    same_copies = [ring_copy(same_ring(step), step) for step in range(1, half_n)]
    other_copies = [ring_copy(other_ring(step), half_n + step) for step in range(half_n)]

    def send_same():
        heed(3)
        for copy in same_copies:
            copy.start()

    def send_other():
        heed(1)
        for copy in other_copies:
            copy.start()
        across.start()

    @pl.when(early)
    def _():
        hear(3, half_n - 1)
        send_same()

    @pl.when(late)
    def _():
        send_other()
        send_halos()
        hear(3, half_n - 1)
        send_same()

    def sweep(load_plane, faces, normal, emit):
        before, cell = load_plane(0), load_plane(1)
        after = load_plane(2)
        diff = [b - a for a, b in zip(before, cell)]
        diff_up = [b - a for a, b in zip(cell, after)]
        left = [c + half_slope(a, b) for a, b, c in zip(diff, diff_up, cell)]

        def face(k, carry):
            cell, diff, left, flux_low = carry
            after = load_plane(k + 3)
            diff_up = [b - a for a, b in zip(cell, after)]
            slope = [half_slope(a, b) for a, b in zip(diff, diff_up)]
            right = [c - s for c, s in zip(cell, slope)]
            flux = double_flux(left, right, normal)
            return after, diff_up, [c + s for c, s in zip(cell, slope)], flux

        carry = face(0, (after, diff_up, left, None))

        def body(k, carry):
            low = carry[3]
            carry = face(k, carry)
            emit(k - 1, [b - a for a, b in zip(low, carry[3])])
            return carry

        lax.fori_loop(1, faces, body, carry)

    @pl.when(not_first)
    def _():
        up.wait_recv()
        down.wait_send()

    @pl.when(not_last)
    def _():
        up.wait_send()
        down.wait_recv()

    for half in range(2):

        def axial_plane(k):
            at = pl.multiple_of(k * width + half * 8, 8)
            return [prim_v[f, pl.ds(at, 8), :] for f in range(8)]

        def axial_emit(k, change):
            at = pl.ds(pl.multiple_of(k * width + half * 8, 8), 8)
            for f in range(8):
                res_ref[f, at, :] = res_ref[f, at, :] - 0.5 * change[f]

        sweep(axial_plane, depth + 1, 2, axial_emit)

    @pl.when(early)
    def _():
        hear(1, half_n)
        send_other()
        pl.when(ahead_waits)(ahead.start)
        pl.when(back_waits)(back.start)

    ahead.wait_recv()
    back.wait_recv()

    def theta_plane(k):
        return [cross_v[f, pl.ds(pl.multiple_of(k * depth, depth), depth), :] for f in range(8)]

    def theta_emit(k, change):
        for f in range(8):
            at = pl.ds(k, depth, stride=width)
            res_ref[f, at, :] = res_ref[f, at, :] - turn * change[f]

    sweep(theta_plane, width + 1, 1, theta_emit)

    ahead.wait_send()
    back.wait_send()

    across.wait()
    cell = [turned_v[f : f + 1, :] for f in range(8)]
    left = [
        cell[f]
        + half_slope(cell[f] - edge_in[f : f + 1, :], turned_v[8 + f : 9 + f, :])
        for f in range(8)
    ]
    face_one = double_flux(left, [turned_v[16 + f : 17 + f, :] for f in range(8)], 0)

    for copy in same_copies + other_copies:
        copy.wait()
    registers = out_v[ring_pos]
    for step in range(1, ring_n):
        registers = registers + in_v[(ring_pos + step) % ring_n]
    mismatch = registers - coarse
    inner = jnp.concatenate([0.5 * v for v in face_one], axis=0)
    for z in range(depth):
        shift = (128 - z * width) % 128
        at = pl.ds(z, 8, stride=depth)
        mis_ref[at, :] = (pltpu.roll(mismatch, shift, 1) if shift else mismatch)[:, :width]
        inner_ref[at, :] = (pltpu.roll(inner, shift, 1) if shift else inner)[:, :width]
    face = (BR * level).astype(F32)
    added = mismatch * (face / (face + 0.5))
    nothing = jnp.zeros((1, 128), F32)
    inner_part, outer_part = [], []
    for f in range(8):
        inner_part += [-face_one[f], face_one[f] * (1.0 / 3.0), nothing, nothing]
        outer_part += [added[f : f + 1], nothing, nothing, nothing]
    corr_v[...] = jnp.concatenate(inner_part + outer_part * 3, axis=0).T

    hits = [(lane < 2) | (lane == BR * depth_of[half]) for half in range(2)]

    def correct(z, _):
        for half in range(2):
            at = pl.ds(pl.multiple_of(z * width + half * 8, 8), 8)
            corr = corr_v[at, :]
            for f in range(8):
                moved = pltpu.roll(corr, 128 - 4 * f, 1) if f else corr
                res_ref[f, at, :] = res_ref[f, at, :] + jnp.where(hits[half], moved, 0.0)
        return 0

    lax.fori_loop(0, depth, correct, 0, unroll=2)


def copy_out(*refs):
    count = len(refs) // 2
    copies = [
        pltpu.make_async_copy(refs[i], refs[count + i], refs[-1].at[i]) for i in range(count)
    ]
    for copy in copies:
        copy.start()
    for copy in copies:
        copy.wait()


def body(mesh_shape, fluid_state, levels, fine_rim, slot_owner, slot_block, slot_count):
    fields, depth, width, radial = fluid_state.shape
    theta_n, gz_n = mesh_shape
    rows = depth * width
    ring_n = theta_n // QUAD
    slots = fine_rim.shape[0]
    sizes = (theta_n, gz_n, depth, width, 2.0 * math.pi / (width * theta_n))
    hbm = pl.BlockSpec(memory_space=pltpu.MemorySpace.HBM)
    vmem = pl.BlockSpec(memory_space=pltpu.MemorySpace.VMEM)
    res, mis, inner = pl.pallas_call(
        functools.partial(kernel, sizes),
        out_shape=(
            jax.ShapeDtypeStruct((fields, rows, radial), F32),
            jax.ShapeDtypeStruct((fields * depth, width), F32),
            jax.ShapeDtypeStruct((fields * depth, width), F32),
        ),
        in_specs=[hbm] * 6,
        out_specs=(vmem, vmem, vmem),
        scratch_shapes=[
            pltpu.VMEM((fields, rows, radial), F32),
            pltpu.VMEM((slots * 2 * fields, 128), F32),
            pltpu.VMEM((fields, rows + 4 * width, radial), F32),
            pltpu.VMEM((fields, rows + 4 * depth, radial), F32),
            pltpu.VMEM((8, 128), F32),
            pltpu.VMEM((8, 128), F32),
            pltpu.VMEM((rows, 128), F32),
            pltpu.VMEM((128, rows), F32),
            pltpu.VMEM((rows, 128), F32),
            pltpu.VMEM((QUAD, slots * fields, 128), F32),
            pltpu.VMEM((ring_n, 8, 128), F32),
            pltpu.VMEM((ring_n, 8, 128), F32),
            pltpu.SMEM((2, 4), jnp.int32),
            pltpu.SMEM(slot_owner.shape, jnp.int32),
            pltpu.SMEM(slot_block.shape, jnp.int32),
            pltpu.SMEM(slot_count.shape, jnp.int32),
            pltpu.SemaphoreType.DMA((6,)),
            pltpu.SemaphoreType.DMA((QUAD,)),
            pltpu.SemaphoreType.DMA((QUAD,)),
            pltpu.SemaphoreType.DMA((ring_n,)),
            pltpu.SemaphoreType.DMA((ring_n,)),
            pltpu.SemaphoreType.DMA((5,)),
            pltpu.SemaphoreType.DMA((5,)),
            pltpu.SemaphoreType.REGULAR((4,)),
        ],
        compiler_params=pltpu.CompilerParams(
            collective_id=0, has_side_effects=True, vmem_limit_bytes=32 * 1024 * 1024
        ),
    )(
        *(
            pltpu.with_memory_space_constraint(v, pltpu.MemorySpace.HBM)
            for v in (
                fluid_state.reshape(fields, rows, radial),
                fine_rim.reshape(slots * 2 * fields, 128),
                levels.T,
                slot_owner,
                slot_block,
                slot_count,
            )
        )
    )
    outs = (res, mis, inner)
    res, mis, inner = pl.pallas_call(
        copy_out,
        out_shape=tuple(jax.ShapeDtypeStruct(v.shape, F32) for v in outs),
        in_specs=[vmem] * 3,
        out_specs=(hbm,) * 3,
        scratch_shapes=[pltpu.SemaphoreType.DMA((3,))],
        compiler_params=pltpu.CompilerParams(vmem_limit_bytes=2 * 1024 * 1024),
    )(*outs)
    return (
        res.reshape(fields, depth, width, radial),
        mis.reshape(fields, depth, width),
        inner.reshape(fields, depth, width),
    )


def solution(mesh):
    return jax.shard_map(
        functools.partial(body, (mesh.shape["theta"], mesh.shape["gz"])),
        mesh=mesh,
        in_specs=(
            P(None, "gz", "theta", None),
            P(None, "theta"),
            P("theta", None, None, "gz"),
            P(),
            P(),
            P(),
        ),
        out_specs=(P(None, "gz", "theta", None), P(None, "gz", "theta"), P(None, "gz", "theta")),
        check_vma=False,
    )
```

```python
import functools
import math

import jax
import jax.numpy as jnp
from jax import lax
from jax.experimental import pallas as pl
from jax.experimental.pallas import tpu as pltpu
from jax.sharding import PartitionSpec as P

BT = 8
BR = 32
GAMMA = 5.0 / 3.0
QUAD = 4
F32 = jnp.float32
MESH = pl.DeviceIdType.MESH


def primitive(cons):
    rho, mr, mt, mz, energy, br, bt, bz = cons
    inv = 1.0 / rho
    vr, vt, vz = mr * inv, mt * inv, mz * inv
    kinetic = mr * vr + mt * vt + mz * vz
    magnetic = br * br + bt * bt + bz * bz
    pressure = (GAMMA - 1.0) * (energy - 0.5 * (kinetic + magnetic))
    return [rho, vr, vt, vz, pressure, br, bt, bz]


def side_state(state, normal):
    rho, pressure = state[0], state[4]
    vel, field = state[1:4], state[5:8]
    mom = [rho * v for v in vel]
    vel_n, field_n = vel[normal], field[normal]
    field_sq = field[0] * field[0] + field[1] * field[1] + field[2] * field[2]
    half_sq = 0.5 * field_sq
    kinetic = 0.5 * (mom[0] * vel[0] + mom[1] * vel[1] + mom[2] * vel[2])
    vel_dot = vel[0] * field[0] + vel[1] * field[1] + vel[2] * field[2]
    total_p = pressure + half_sq
    energy = pressure * (1.0 / (GAMMA - 1.0)) + kinetic + half_sq
    flux = [mom[normal]]
    for comp in range(3):
        term = mom[comp] * vel_n - field[comp] * field_n
        flux.append(term + total_p if comp == normal else term)
    flux.append((energy + total_p) * vel_n - field_n * vel_dot)
    for comp in range(3):
        flux.append(None if comp == normal else vel_n * field[comp] - field_n * vel[comp])
    fast = GAMMA * pressure + field_sq
    signal = jnp.abs(vel_n) + fast * lax.rsqrt(fast * rho)
    return [rho] + mom + [energy] + list(field), flux, signal


def double_flux(left, right, normal):
    cons_l, flux_l, signal_l = side_state(left, normal)
    cons_r, flux_r, signal_r = side_state(right, normal)
    top = jnp.maximum(signal_l, signal_r)
    out = []
    for ul, ur, fl, fr in zip(cons_l, cons_r, flux_l, flux_r):
        if fl is None:
            out.append(top * (ul - ur))
        else:
            out.append((fl + fr) - top * (ur - ul))
    return out


def half_slope(lower, upper):
    low, high = jnp.minimum(lower, upper), jnp.maximum(lower, upper)
    return 0.5 * (jnp.maximum(low, 0.0) + jnp.minimum(high, 0.0))


def kernel(
    sizes,
    x_hbm, fine_hbm, levels_hbm, owner_hbm, block_hbm, count_hbm,
    res_ref, mis_ref, inner_ref,
    x_v, fine_v, prim_v, cross_v, edge_v, edge_in, packed_v, turned_v, corr_v,
    quad_v, out_v, in_v,
    levels_s, owner_s, block_s, count_s,
    load_sem, quad_send, quad_recv, ring_send, ring_recv, halo_send, halo_recv, news_sem,
):
    theta_n, gz_n, depth, width, dtheta = sizes
    rows = depth * width
    ring_n = theta_n // QUAD
    theta = lax.axis_index("theta")
    gz = lax.axis_index("gz")
    ring_pos, quad_pos = theta // QUAD, theta % QUAD

    def load(src, dst, sem):
        return pltpu.make_async_copy(src, dst, load_sem.at[sem])

    loads = [
        load(fine_hbm, fine_v, 0),
        load(x_hbm, x_v, 1),
        load(levels_hbm, levels_s, 2),
        load(owner_hbm, owner_s, 3),
        load(block_hbm, block_s, 4),
        load(count_hbm, count_s, 5),
    ]
    for item in loads:
        item.start()

    barrier = pltpu.get_barrier_semaphore()
    half_n = ring_n // 2
    early = ring_pos < half_n
    late = jnp.logical_not(early)
    soon = ring_pos < half_n // 2
    later = jnp.logical_not(soon)
    half_at = ring_pos // half_n * half_n
    core_zero = quad_pos % 2 == 0
    not_start, not_end = ring_pos > half_at, ring_pos < half_at + half_n - 1
    ring_near = not_start.astype(jnp.int32) + not_end.astype(jnp.int32)

    def signal(sem, t, g):
        pl.semaphore_signal(sem, inc=1, device_id={"theta": t, "gz": g}, device_id_type=MESH)

    def same_ring(step):
        return half_at + (ring_pos - half_at + step) % half_n

    def other_ring(step):
        return half_n - half_at + (ring_pos - half_at + step) % half_n

    def hear(role, count):
        @pl.when(quad_pos == role)
        def _():
            pl.semaphore_wait(barrier, count)
            for step in range(1, QUAD):
                signal(news_sem.at[role], ring_pos * QUAD + (role + step) % QUAD, gz)

    def heed(role):
        @pl.when(quad_pos != role)
        def _():
            pl.semaphore_wait(news_sem.at[role], 1)

    @pl.when(quad_pos != 0)
    def _():
        signal(barrier, ring_pos * QUAD, gz)

    @pl.when(later & (quad_pos != 2))
    def _():
        signal(barrier, ring_pos * QUAD + 2, gz)

    lane = lax.broadcasted_iota(jnp.int32, (8, 128), 1)
    lane_block = (lane % width) // BT

    loads[0].wait()
    sides = [
        [fine_v[pl.ds(side * 8 + var, 8, stride=16), :] for var in range(8)] for side in (0, 1)
    ]
    fine_flux = jnp.concatenate(double_flux(sides[0], sides[1], 0), axis=0)
    src = lax.broadcasted_iota(jnp.int32, (128, 128), 0)
    dst = lax.broadcasted_iota(jnp.int32, (128, 128), 1)
    pairing = jnp.where(
        (src // width == dst // width) & ((src % width) // 2 == dst % BT), 0.125, 0.0
    ).astype(F32)
    partial = jnp.dot(
        fine_flux, pairing, precision=lax.Precision.HIGHEST, preferred_element_type=F32
    )
    for var in range(8):
        rows_var = partial[var * 8 : var * 8 + 8]
        pair = jnp.where(lane_block == 0, rows_var, pltpu.roll(rows_var, 4, 0))
        quad_v[quad_pos, pl.ds(var, 4, stride=8), :] = pair[0:4]

    def remote(src, dst, send, recv, t, g):
        return pltpu.make_async_remote_copy(
            src_ref=src, dst_ref=dst, send_sem=send, recv_sem=recv,
            device_id={"theta": t, "gz": g}, device_id_type=MESH,
        )

    partners = [quad_pos + 1 - 2 * (quad_pos % 2), (quad_pos + 2) % QUAD, QUAD - 1 - quad_pos]
    quad_copies = [
        remote(
            quad_v.at[quad_pos], quad_v.at[quad_pos], quad_send.at[i], quad_recv.at[i],
            ring_pos * QUAD + partner, gz,
        )
        for i, partner in enumerate(partners)
    ]
    gz_next, gz_back = (gz + 1) % gz_n, (gz + gz_n - 1) % gz_n

    def greet_near():
        signal(barrier, theta, gz_next)
        signal(barrier, theta, gz_back)
        for there, r in ((not_start, ring_pos - 1), (not_end, ring_pos + 1)):
            role = jnp.where((r >= 0) & (r < half_n // 2), 2, 3)
            pl.when(there)(functools.partial(signal, barrier, r * QUAD + role, gz))

    def start_quad():
        pl.when(soon)(functools.partial(hear, 0, QUAD - 1))

        @pl.when(later & core_zero)
        def _():
            pl.semaphore_wait(barrier, QUAD - 1)
            signal(news_sem.at[0], theta + 1, gz)

        @pl.when((soon & (quad_pos != 0)) | (later & jnp.logical_not(core_zero)))
        def _():
            pl.semaphore_wait(news_sem.at[0], 1)

        for i in (1, 2, 0):
            quad_copies[i].start()

        @pl.when(quad_pos == 1)
        def _():
            for step in range(half_n):
                signal(barrier, other_ring(step) * QUAD + 1, gz)

        pl.when(soon & (quad_pos == 2))(greet_near)

        @pl.when(quad_pos == 3)
        def _():
            pl.when(later)(greet_near)
            for step in range(1, half_n):
                signal(barrier, same_ring(step) * QUAD + 3, gz)

    upper = quad_pos >= QUAD // 2
    pl.when(upper)(start_quad)

    loads[1].wait()

    def to_primitive(z, _):
        at = pl.multiple_of(z * width, width)
        for half in range(2):
            prims = primitive([x_v[f, pl.ds(at + half * 8, 8), :] for f in range(8)])
            for f, value in enumerate(prims):
                prim_v[f, pl.ds(at + 2 * width + half * 8, 8), :] = value
                cross_v[f, pl.ds((2 + half * 8) * depth + z, 8, stride=depth), :] = value
        return 0

    lax.fori_loop(0, depth, to_primitive, 0)

    pl.when(jnp.logical_not(upper))(start_quad)

    radius = lane.astype(F32) + 0.5
    inv_radius = 1.0 / radius
    inward = jnp.where(lane == 1, 0.0, 0.5 * (radius - 0.5) * inv_radius)
    outward = jnp.where(lane == 0, 0.0, 0.5 * (radius + 0.5) * inv_radius)
    turn = inv_radius * (0.5 / dtheta)
    last = lane == 127
    spot = jnp.where(lane >= BR, lane % BR, -1)

    def radial(z, _):
        for half in range(2):
            at = pl.multiple_of(z * width + half * 8, 8)
            left, right = [], []
            cell = [prim_v[f, pl.ds(at + 2 * width, 8), :] for f in range(8)]
            packed = jnp.zeros((8, 128), F32)
            for f in range(8):
                mid = cell[f]
                lower = mid - pltpu.roll(mid, 1, 1)
                upper = jnp.where(last, 0.0, pltpu.roll(lower, 127, 1))
                slope = half_slope(lower, upper)
                left.append(mid + slope)
                right.append(jnp.where(last, mid, pltpu.roll(mid - slope, 127, 1)))
                packed = jnp.where(lane == f, pltpu.roll(mid, f, 1) if f else mid, packed)
                packed = jnp.where(lane == f + 8, pltpu.roll(upper, f + 8, 1), packed)
                packed = jnp.where(lane == f + 16, pltpu.roll(right[f], f + 16, 1), packed)
            flux = double_flux(left, right, 0)
            rho, vr, vt, _, pressure, br, bt, bz = cell
            out = [inward * pltpu.roll(v, 1, 1) - outward * v for v in flux]
            field_sq = br * br + bt * bt + bz * bz
            out[1] = out[1] + inv_radius * (rho * vt * vt + pressure + 0.5 * field_sq - bt * bt)
            out[2] = out[2] - inv_radius * (rho * vr * vt - br * bt)
            out[6] = out[6] + inv_radius * (vr * bt - vt * br)
            for f in range(8):
                res_ref[f, pl.ds(at, 8), :] = out[f]
                packed = jnp.where(spot == f, pltpu.roll(flux[f], f + 1, 1), packed)
            packed_v[pl.ds(at, 8), :] = packed
        return 0

    lax.fori_loop(0, depth, radial, 0)
    turned_v[...] = packed_v[...].T
    row = lax.broadcasted_iota(jnp.int32, (8, 128), 0)
    flip = (row == 1) | (row == 2) | (row == 5) | (row == 6)
    edge_v[...] = jnp.where(flip, -turned_v[0:8, :], turned_v[0:8, :])

    loads[2].wait()
    depth_of = [levels_s[b, 0] + levels_s[b, 1] + levels_s[b, 2] + levels_s[b, 3] for b in range(2)]
    level = jnp.where(lane_block == 0, depth_of[0], depth_of[1])
    coarse = 0.5 * jnp.where(
        level == 1,
        turned_v[BR : BR + 8, :],
        jnp.where(level == 2, turned_v[2 * BR : 2 * BR + 8, :], turned_v[3 * BR : 3 * BR + 8, :]),
    )

    across = remote(
        edge_v, edge_in, halo_send.at[0], halo_recv.at[0], (theta + theta_n // 2) % theta_n, gz
    )
    two_z, two_t = 2 * width, 2 * depth
    up = remote(
        prim_v.at[:, pl.ds(rows, two_z)], prim_v.at[:, pl.ds(0, two_z)],
        halo_send.at[1], halo_recv.at[1], theta, (gz + 1) % gz_n,
    )
    down = remote(
        prim_v.at[:, pl.ds(two_z, two_z)], prim_v.at[:, pl.ds(rows + two_z, two_z)],
        halo_send.at[2], halo_recv.at[2], theta, (gz + gz_n - 1) % gz_n,
    )
    not_last, not_first = gz < gz_n - 1, gz > 0
    ahead = remote(
        cross_v.at[:, pl.ds(rows, two_t)], cross_v.at[:, pl.ds(0, two_t)],
        halo_send.at[3], halo_recv.at[3], (theta + 1) % theta_n, gz,
    )
    back = remote(
        cross_v.at[:, pl.ds(two_t, two_t)], cross_v.at[:, pl.ds(rows + two_t, two_t)],
        halo_send.at[4], halo_recv.at[4], (theta + theta_n - 1) % theta_n, gz,
    )

    ahead_far = (theta + 1) % (theta_n // 2) == 0
    back_far = theta % (theta_n // 2) == 0

    def send_halos():
        pl.when(jnp.logical_not(ahead_far))(ahead.start)
        pl.when(jnp.logical_not(back_far))(back.start)
        pl.when(not_last)(up.start)
        pl.when(not_first)(down.start)

    @pl.when(gz == 0)
    def _():
        for f in range(8):
            plane = prim_v[f, pl.ds(two_z, width), :]
            prim_v[f, pl.ds(0, width), :] = plane
            prim_v[f, pl.ds(width, width), :] = plane

    @pl.when(gz == gz_n - 1)
    def _():
        for f in range(8):
            plane = prim_v[f, pl.ds(rows + width, width), :]
            prim_v[f, pl.ds(rows + 2 * width, width), :] = plane
            prim_v[f, pl.ds(rows + 3 * width, width), :] = plane

    @pl.when(soon)
    def _():
        hear(2, 2 + ring_near)
        heed(2)
        send_halos()

    pl.when(late)(functools.partial(hear, 1, half_n))

    for item in loads[3:]:
        item.wait()

    def spread(base, step, totals):
        device, k = base + step // 4, step % 4
        both = quad_v[device, pl.ds(pl.multiple_of(k * 8, 8), 8), :]
        values = (
            jnp.where(lane_block == 0, both, pltpu.roll(both, BT, 1)),
            jnp.where(lane_block == 1, both, pltpu.roll(both, 128 - BT, 1)),
        )
        for slot, value in zip((k, k + 4), values):
            index = (ring_pos * QUAD + device) * 8 + slot
            live = slot < count_s[ring_pos * QUAD + device]
            code = jnp.where(live, owner_s[index] * 2 + block_s[index], -1)
            relative = code - 2 * quad_pos - lane_block
            totals = tuple(
                total + jnp.where(relative == 2 * QUAD * z, value, 0.0)
                for z, total in enumerate(totals)
            )
        return totals

    totals = tuple(jnp.zeros((8, 128), F32) for _ in range(ring_n))
    own = quad_pos // 2 * 2
    quad_copies[0].wait()
    totals = lax.fori_loop(0, 8, functools.partial(spread, own), totals)
    quad_copies[1].wait()
    quad_copies[2].wait()
    totals = lax.fori_loop(0, 8, functools.partial(spread, 2 - own), totals)
    for k in range(ring_n):
        out_v[k] = totals[k]

    def ring_copy(to, slot):
        return remote(
            out_v.at[to], in_v.at[ring_pos], ring_send.at[slot], ring_recv.at[slot],
            to * QUAD + quad_pos, gz,
        )

    same_copies = [ring_copy(same_ring(step), step) for step in range(1, half_n)]
    other_copies = [ring_copy(other_ring(step), half_n + step) for step in range(half_n)]

    def send_same():
        for copy in same_copies:
            copy.start()

    def send_other():
        heed(1)
        pl.when(ahead_far)(ahead.start)
        across.start()
        for copy in other_copies:
            copy.start()
        pl.when(back_far)(back.start)

    @pl.when(early)
    def _():
        hear(3, half_n - 1 + jnp.where(soon, 0, 2 + ring_near))
        heed(3)
        send_same()
        pl.when(later)(send_halos)
        hear(1, half_n)
        send_other()

    @pl.when(late)
    def _():
        send_other()
        hear(3, half_n - 1 + 2 + ring_near)
        heed(3)
        send_halos()
        send_same()

    def sweep(load_plane, faces, normal, emit):
        before, cell = load_plane(0), load_plane(1)
        after = load_plane(2)
        diff = [b - a for a, b in zip(before, cell)]
        diff_up = [b - a for a, b in zip(cell, after)]
        left = [c + half_slope(a, b) for a, b, c in zip(diff, diff_up, cell)]

        def face(k, carry):
            cell, diff, left, flux_low = carry
            after = load_plane(k + 3)
            diff_up = [b - a for a, b in zip(cell, after)]
            slope = [half_slope(a, b) for a, b in zip(diff, diff_up)]
            right = [c - s for c, s in zip(cell, slope)]
            flux = double_flux(left, right, normal)
            return after, diff_up, [c + s for c, s in zip(cell, slope)], flux

        carry = face(0, (after, diff_up, left, None))

        def body(k, carry):
            low = carry[3]
            carry = face(k, carry)
            emit(k - 1, [b - a for a, b in zip(low, carry[3])])
            return carry

        lax.fori_loop(1, faces, body, carry)

    @pl.when(not_first)
    def _():
        up.wait_recv()
        down.wait_send()

    @pl.when(not_last)
    def _():
        up.wait_send()
        down.wait_recv()

    for half in range(2):

        def axial_plane(k):
            at = pl.multiple_of(k * width + half * 8, 8)
            return [prim_v[f, pl.ds(at, 8), :] for f in range(8)]

        def axial_emit(k, change):
            at = pl.ds(pl.multiple_of(k * width + half * 8, 8), 8)
            for f in range(8):
                res_ref[f, at, :] = res_ref[f, at, :] - 0.5 * change[f]

        sweep(axial_plane, depth + 1, 2, axial_emit)

    back.wait_recv()

    def theta_plane(k):
        return [cross_v[f, pl.ds(pl.multiple_of(k * depth, depth), depth), :] for f in range(8)]

    def theta_emit(k, change):
        for f in range(8):
            at = pl.ds(k, depth, stride=width)
            res_ref[f, at, :] = res_ref[f, at, :] - turn * change[f]

    sweep(lambda k: theta_plane(k + 2), width - 1, 1, lambda k, change: theta_emit(k + 2, change))
    ahead.wait_recv()
    sweep(theta_plane, 3, 1, theta_emit)

    ahead.wait_send()
    back.wait_send()

    across.wait()
    cell = [turned_v[f : f + 1, :] for f in range(8)]
    left = [
        cell[f]
        + half_slope(cell[f] - edge_in[f : f + 1, :], turned_v[8 + f : 9 + f, :])
        for f in range(8)
    ]
    face_one = double_flux(left, [turned_v[16 + f : 17 + f, :] for f in range(8)], 0)

    for copy in same_copies + other_copies:
        copy.wait()
    registers = out_v[ring_pos]
    for step in range(1, ring_n):
        registers = registers + in_v[(ring_pos + step) % ring_n]
    mismatch = registers - coarse
    inner = jnp.concatenate([0.5 * v for v in face_one], axis=0)
    for z in range(depth):
        shift = (128 - z * width) % 128
        at = pl.ds(z, 8, stride=depth)
        mis_ref[at, :] = (pltpu.roll(mismatch, shift, 1) if shift else mismatch)[:, :width]
        inner_ref[at, :] = (pltpu.roll(inner, shift, 1) if shift else inner)[:, :width]
    face = (BR * level).astype(F32)
    added = mismatch * (face / (face + 0.5))
    nothing = jnp.zeros((1, 128), F32)
    inner_part, outer_part = [], []
    for f in range(8):
        inner_part += [-face_one[f], face_one[f] * (1.0 / 3.0), nothing, nothing]
        outer_part += [added[f : f + 1], nothing, nothing, nothing]
    corr_v[...] = jnp.concatenate(inner_part + outer_part * 3, axis=0).T

    hits = [(lane < 2) | (lane == BR * depth_of[half]) for half in range(2)]

    def correct(z, _):
        for half in range(2):
            at = pl.ds(pl.multiple_of(z * width + half * 8, 8), 8)
            corr = corr_v[at, :]
            for f in range(8):
                moved = pltpu.roll(corr, 128 - 4 * f, 1) if f else corr
                res_ref[f, at, :] = res_ref[f, at, :] + jnp.where(hits[half], moved, 0.0)
        return 0

    lax.fori_loop(0, depth, correct, 0, unroll=True)


def copy_out(*refs):
    count = len(refs) // 2
    copies = [
        pltpu.make_async_copy(refs[i], refs[count + i], refs[-1].at[i]) for i in range(count)
    ]
    for copy in copies:
        copy.start()
    for copy in copies:
        copy.wait()


def body(mesh_shape, fluid_state, levels, fine_rim, slot_owner, slot_block, slot_count):
    fields, depth, width, radial = fluid_state.shape
    theta_n, gz_n = mesh_shape
    rows = depth * width
    ring_n = theta_n // QUAD
    slots = fine_rim.shape[0]
    sizes = (theta_n, gz_n, depth, width, 2.0 * math.pi / (width * theta_n))
    hbm = pl.BlockSpec(memory_space=pltpu.MemorySpace.HBM)
    vmem = pl.BlockSpec(memory_space=pltpu.MemorySpace.VMEM)
    res, mis, inner = pl.pallas_call(
        functools.partial(kernel, sizes),
        out_shape=(
            jax.ShapeDtypeStruct((fields, rows, radial), F32),
            jax.ShapeDtypeStruct((fields * depth, width), F32),
            jax.ShapeDtypeStruct((fields * depth, width), F32),
        ),
        in_specs=[hbm] * 6,
        out_specs=(vmem, vmem, vmem),
        scratch_shapes=[
            pltpu.VMEM((fields, rows, radial), F32),
            pltpu.VMEM((slots * 2 * fields, 128), F32),
            pltpu.VMEM((fields, rows + 4 * width, radial), F32),
            pltpu.VMEM((fields, rows + 4 * depth, radial), F32),
            pltpu.VMEM((8, 128), F32),
            pltpu.VMEM((8, 128), F32),
            pltpu.VMEM((rows, 128), F32),
            pltpu.VMEM((128, rows), F32),
            pltpu.VMEM((rows, 128), F32),
            pltpu.VMEM((QUAD, slots * fields // 2, 128), F32),
            pltpu.VMEM((ring_n, 8, 128), F32),
            pltpu.VMEM((ring_n, 8, 128), F32),
            pltpu.SMEM((2, 4), jnp.int32),
            pltpu.SMEM(slot_owner.shape, jnp.int32),
            pltpu.SMEM(slot_block.shape, jnp.int32),
            pltpu.SMEM(slot_count.shape, jnp.int32),
            pltpu.SemaphoreType.DMA((6,)),
            pltpu.SemaphoreType.DMA((QUAD,)),
            pltpu.SemaphoreType.DMA((QUAD,)),
            pltpu.SemaphoreType.DMA((ring_n,)),
            pltpu.SemaphoreType.DMA((ring_n,)),
            pltpu.SemaphoreType.DMA((5,)),
            pltpu.SemaphoreType.DMA((5,)),
            pltpu.SemaphoreType.REGULAR((4,)),
        ],
        compiler_params=pltpu.CompilerParams(
            collective_id=0, has_side_effects=True, vmem_limit_bytes=32 * 1024 * 1024
        ),
    )(
        *(
            pltpu.with_memory_space_constraint(v, pltpu.MemorySpace.HBM)
            for v in (
                fluid_state.reshape(fields, rows, radial),
                fine_rim.reshape(slots * 2 * fields, 128),
                levels.T,
                slot_owner,
                slot_block,
                slot_count,
            )
        )
    )
    outs = (res, mis, inner)
    res, mis, inner = pl.pallas_call(
        copy_out,
        out_shape=tuple(jax.ShapeDtypeStruct(v.shape, F32) for v in outs),
        in_specs=[vmem] * 3,
        out_specs=(hbm,) * 3,
        scratch_shapes=[pltpu.SemaphoreType.DMA((3,))],
        compiler_params=pltpu.CompilerParams(vmem_limit_bytes=2 * 1024 * 1024),
    )(*outs)
    return (
        res.reshape(fields, depth, width, radial),
        mis.reshape(fields, depth, width),
        inner.reshape(fields, depth, width),
    )


def solution(mesh):
    return jax.shard_map(
        functools.partial(body, (mesh.shape["theta"], mesh.shape["gz"])),
        mesh=mesh,
        in_specs=(
            P(None, "gz", "theta", None),
            P(None, "theta"),
            P("theta", None, None, "gz"),
            P(),
            P(),
            P(),
        ),
        out_specs=(P(None, "gz", "theta", None), P(None, "gz", "theta"), P(None, "gz", "theta")),
        check_vma=False,
    )
```

```python
import functools
import math

import jax
import jax.numpy as jnp
from jax import lax
from jax.experimental import pallas as pl
from jax.experimental.pallas import tpu as pltpu
from jax.sharding import PartitionSpec as P

BT = 8
BR = 32
GAMMA = 5.0 / 3.0
QUAD = 4
F32 = jnp.float32
MESH = pl.DeviceIdType.MESH


def primitive(cons):
    rho, mr, mt, mz, energy, br, bt, bz = cons
    inv = 1.0 / rho
    vr, vt, vz = mr * inv, mt * inv, mz * inv
    kinetic = mr * vr + mt * vt + mz * vz
    magnetic = br * br + bt * bt + bz * bz
    pressure = (GAMMA - 1.0) * (energy - 0.5 * (kinetic + magnetic))
    return [rho, vr, vt, vz, pressure, br, bt, bz]


def side_state(state, normal):
    rho, pressure = state[0], state[4]
    vel, field = state[1:4], state[5:8]
    mom = [rho * v for v in vel]
    vel_n, field_n = vel[normal], field[normal]
    field_sq = field[0] * field[0] + field[1] * field[1] + field[2] * field[2]
    half_sq = 0.5 * field_sq
    kinetic = 0.5 * (mom[0] * vel[0] + mom[1] * vel[1] + mom[2] * vel[2])
    vel_dot = vel[0] * field[0] + vel[1] * field[1] + vel[2] * field[2]
    total_p = pressure + half_sq
    energy = pressure * (1.0 / (GAMMA - 1.0)) + kinetic + half_sq
    flux = [mom[normal]]
    for comp in range(3):
        term = mom[comp] * vel_n - field[comp] * field_n
        flux.append(term + total_p if comp == normal else term)
    flux.append((energy + total_p) * vel_n - field_n * vel_dot)
    for comp in range(3):
        flux.append(None if comp == normal else vel_n * field[comp] - field_n * vel[comp])
    fast = GAMMA * pressure + field_sq
    signal = jnp.abs(vel_n) + fast * lax.rsqrt(fast * rho)
    return [rho] + mom + [energy] + list(field), flux, signal


def double_flux(left, right, normal):
    cons_l, flux_l, signal_l = side_state(left, normal)
    cons_r, flux_r, signal_r = side_state(right, normal)
    top = jnp.maximum(signal_l, signal_r)
    out = []
    for ul, ur, fl, fr in zip(cons_l, cons_r, flux_l, flux_r):
        if fl is None:
            out.append(top * (ul - ur))
        else:
            out.append((fl + fr) - top * (ur - ul))
    return out


def half_slope(lower, upper):
    low, high = jnp.minimum(lower, upper), jnp.maximum(lower, upper)
    return 0.5 * (jnp.maximum(low, 0.0) + jnp.minimum(high, 0.0))


def kernel(
    sizes,
    x_hbm, fine_hbm, levels_hbm, owner_hbm, block_hbm, count_hbm,
    res_ref, mis_ref, inner_ref,
    x_v, fine_v, prim_v, cross_v, edge_v, edge_in, packed_v, turned_v, corr_v,
    quad_v, out_v, in_v,
    levels_s, owner_s, block_s, count_s,
    load_sem, quad_send, quad_recv, ring_send, ring_recv, halo_send, halo_recv, news_sem,
):
    theta_n, gz_n, depth, width, dtheta = sizes
    rows = depth * width
    ring_n = theta_n // QUAD
    theta = lax.axis_index("theta")
    gz = lax.axis_index("gz")
    ring_pos, quad_pos = theta // QUAD, theta % QUAD

    def load(src, dst, sem):
        return pltpu.make_async_copy(src, dst, load_sem.at[sem])

    loads = [
        load(fine_hbm, fine_v, 0),
        load(x_hbm, x_v, 1),
        load(levels_hbm, levels_s, 2),
        load(owner_hbm, owner_s, 3),
        load(block_hbm, block_s, 4),
        load(count_hbm, count_s, 5),
    ]
    for item in loads:
        item.start()

    barrier = pltpu.get_barrier_semaphore()
    half_n = ring_n // 2
    early = ring_pos < half_n
    late = jnp.logical_not(early)
    soon = ring_pos < half_n // 2
    later = jnp.logical_not(soon)
    half_at = ring_pos // half_n * half_n
    core_zero = quad_pos % 2 == 0
    not_start, not_end = ring_pos > half_at, ring_pos < half_at + half_n - 1
    ring_near = not_start.astype(jnp.int32) + not_end.astype(jnp.int32)

    def signal(sem, t, g):
        pl.semaphore_signal(sem, inc=1, device_id={"theta": t, "gz": g}, device_id_type=MESH)

    def same_ring(step):
        return half_at + (ring_pos - half_at + step) % half_n

    def other_ring(step):
        return half_n - half_at + (ring_pos - half_at + step) % half_n

    def hear(role, count):
        @pl.when(quad_pos == role)
        def _():
            pl.semaphore_wait(barrier, count)
            for step in range(1, QUAD):
                signal(news_sem.at[role], ring_pos * QUAD + (role + step) % QUAD, gz)

    def heed(role):
        @pl.when(quad_pos != role)
        def _():
            pl.semaphore_wait(news_sem.at[role], 1)

    @pl.when(quad_pos != 0)
    def _():
        signal(barrier, ring_pos * QUAD, gz)

    @pl.when(later & (quad_pos != 2))
    def _():
        signal(barrier, ring_pos * QUAD + 2, gz)

    lane = lax.broadcasted_iota(jnp.int32, (8, 128), 1)
    lane_block = (lane % width) // BT

    loads[0].wait()
    sides = [
        [fine_v[pl.ds(side * 8 + var, 8, stride=16), :] for var in range(8)] for side in (0, 1)
    ]
    fine_flux = jnp.concatenate(double_flux(sides[0], sides[1], 0), axis=0)
    src = lax.broadcasted_iota(jnp.int32, (128, 128), 0)
    dst = lax.broadcasted_iota(jnp.int32, (128, 128), 1)
    pairing = jnp.where(
        (src // width == dst // width) & ((src % width) // 2 == dst % BT), 0.125, 0.0
    ).astype(F32)
    partial = jnp.dot(
        fine_flux, pairing, precision=lax.Precision.HIGHEST, preferred_element_type=F32
    )
    for var in range(8):
        rows_var = partial[var * 8 : var * 8 + 8]
        pair = jnp.where(lane_block == 0, rows_var, pltpu.roll(rows_var, 4, 0))
        quad_v[quad_pos, pl.ds(var, 4, stride=8), :] = pair[0:4]

    def remote(src, dst, send, recv, t, g):
        return pltpu.make_async_remote_copy(
            src_ref=src, dst_ref=dst, send_sem=send, recv_sem=recv,
            device_id={"theta": t, "gz": g}, device_id_type=MESH,
        )

    partners = [quad_pos + 1 - 2 * (quad_pos % 2), (quad_pos + 2) % QUAD, QUAD - 1 - quad_pos]
    quad_copies = [
        remote(
            quad_v.at[quad_pos], quad_v.at[quad_pos], quad_send.at[i], quad_recv.at[i],
            ring_pos * QUAD + partner, gz,
        )
        for i, partner in enumerate(partners)
    ]
    gz_next, gz_back = (gz + 1) % gz_n, (gz + gz_n - 1) % gz_n

    def greet_near():
        signal(barrier, theta, gz_next)
        signal(barrier, theta, gz_back)
        for there, r in ((not_start, ring_pos - 1), (not_end, ring_pos + 1)):
            role = jnp.where((r >= 0) & (r < half_n // 2), 2, 3)
            pl.when(there)(functools.partial(signal, barrier, r * QUAD + role, gz))

    def start_quad():
        pl.when(soon)(functools.partial(hear, 0, QUAD - 1))

        @pl.when(later & core_zero)
        def _():
            pl.semaphore_wait(barrier, QUAD - 1)
            signal(news_sem.at[0], theta + 1, gz)

        @pl.when((soon & (quad_pos != 0)) | (later & jnp.logical_not(core_zero)))
        def _():
            pl.semaphore_wait(news_sem.at[0], 1)

        for i in (1, 2, 0):
            quad_copies[i].start()

        @pl.when(quad_pos == 1)
        def _():
            for step in range(half_n):
                signal(barrier, other_ring(step) * QUAD + 1, gz)

        pl.when(soon & (quad_pos == 2))(greet_near)

        @pl.when(quad_pos == 3)
        def _():
            pl.when(later)(greet_near)
            for step in range(1, half_n):
                signal(barrier, same_ring(step) * QUAD + 3, gz)

    upper = quad_pos >= QUAD // 2
    pl.when(upper)(start_quad)

    loads[1].wait()

    def to_primitive(z, _):
        at = pl.multiple_of(z * width, width)
        for half in range(2):
            prims = primitive([x_v[f, pl.ds(at + half * 8, 8), :] for f in range(8)])
            for f, value in enumerate(prims):
                prim_v[f, pl.ds(at + 2 * width + half * 8, 8), :] = value
                cross_v[f, pl.ds((2 + half * 8) * depth + z, 8, stride=depth), :] = value
        return 0

    lax.fori_loop(0, depth, to_primitive, 0)

    pl.when(jnp.logical_not(upper))(start_quad)

    radius = lane.astype(F32) + 0.5
    inv_radius = 1.0 / radius
    inward = jnp.where(lane == 1, 0.0, 0.5 * (radius - 0.5) * inv_radius)
    outward = jnp.where(lane == 0, 0.0, 0.5 * (radius + 0.5) * inv_radius)
    turn = inv_radius * (0.5 / dtheta)
    last = lane == 127
    spot = jnp.where(lane >= BR, lane % BR, -1)

    def radial(z, _):
        for half in range(2):
            at = pl.multiple_of(z * width + half * 8, 8)
            left, right = [], []
            cell = [prim_v[f, pl.ds(at + 2 * width, 8), :] for f in range(8)]
            packed = jnp.zeros((8, 128), F32)
            for f in range(8):
                mid = cell[f]
                lower = mid - pltpu.roll(mid, 1, 1)
                upper = jnp.where(last, 0.0, pltpu.roll(lower, 127, 1))
                slope = half_slope(lower, upper)
                left.append(mid + slope)
                right.append(jnp.where(last, mid, pltpu.roll(mid - slope, 127, 1)))
                packed = jnp.where(lane == f, pltpu.roll(mid, f, 1) if f else mid, packed)
                packed = jnp.where(lane == f + 8, pltpu.roll(upper, f + 8, 1), packed)
                packed = jnp.where(lane == f + 16, pltpu.roll(right[f], f + 16, 1), packed)
            flux = double_flux(left, right, 0)
            rho, vr, vt, _, pressure, br, bt, bz = cell
            out = [inward * pltpu.roll(v, 1, 1) - outward * v for v in flux]
            field_sq = br * br + bt * bt + bz * bz
            out[1] = out[1] + inv_radius * (rho * vt * vt + pressure + 0.5 * field_sq - bt * bt)
            out[2] = out[2] - inv_radius * (rho * vr * vt - br * bt)
            out[6] = out[6] + inv_radius * (vr * bt - vt * br)
            for f in range(8):
                res_ref[f, pl.ds(at, 8), :] = out[f]
                packed = jnp.where(spot == f, pltpu.roll(flux[f], f + 1, 1), packed)
            packed_v[pl.ds(at, 8), :] = packed
        return 0

    lax.fori_loop(0, depth, radial, 0)
    turned_v[...] = packed_v[...].T
    row = lax.broadcasted_iota(jnp.int32, (8, 128), 0)
    flip = (row == 1) | (row == 2) | (row == 5) | (row == 6)
    edge_v[...] = jnp.where(flip, -turned_v[0:8, :], turned_v[0:8, :])

    loads[2].wait()
    depth_of = [levels_s[b, 0] + levels_s[b, 1] + levels_s[b, 2] + levels_s[b, 3] for b in range(2)]
    level = jnp.where(lane_block == 0, depth_of[0], depth_of[1])
    coarse = 0.5 * jnp.where(
        level == 1,
        turned_v[BR : BR + 8, :],
        jnp.where(level == 2, turned_v[2 * BR : 2 * BR + 8, :], turned_v[3 * BR : 3 * BR + 8, :]),
    )

    across = remote(
        edge_v, edge_in, halo_send.at[0], halo_recv.at[0], (theta + theta_n // 2) % theta_n, gz
    )
    two_z, two_t = 2 * width, 2 * depth
    up = remote(
        prim_v.at[:, pl.ds(rows, two_z)], prim_v.at[:, pl.ds(0, two_z)],
        halo_send.at[1], halo_recv.at[1], theta, (gz + 1) % gz_n,
    )
    down = remote(
        prim_v.at[:, pl.ds(two_z, two_z)], prim_v.at[:, pl.ds(rows + two_z, two_z)],
        halo_send.at[2], halo_recv.at[2], theta, (gz + gz_n - 1) % gz_n,
    )
    not_last, not_first = gz < gz_n - 1, gz > 0
    ahead = remote(
        cross_v.at[:, pl.ds(rows, two_t)], cross_v.at[:, pl.ds(0, two_t)],
        halo_send.at[3], halo_recv.at[3], (theta + 1) % theta_n, gz,
    )
    back = remote(
        cross_v.at[:, pl.ds(two_t, two_t)], cross_v.at[:, pl.ds(rows + two_t, two_t)],
        halo_send.at[4], halo_recv.at[4], (theta + theta_n - 1) % theta_n, gz,
    )

    ahead_far = (theta + 1) % (theta_n // 2) == 0
    back_far = theta % (theta_n // 2) == 0

    def send_halos():
        pl.when(jnp.logical_not(ahead_far))(ahead.start)
        pl.when(jnp.logical_not(back_far))(back.start)
        pl.when(not_last)(up.start)
        pl.when(not_first)(down.start)

    @pl.when(gz == 0)
    def _():
        for f in range(8):
            plane = prim_v[f, pl.ds(two_z, width), :]
            prim_v[f, pl.ds(0, width), :] = plane
            prim_v[f, pl.ds(width, width), :] = plane

    @pl.when(gz == gz_n - 1)
    def _():
        for f in range(8):
            plane = prim_v[f, pl.ds(rows + width, width), :]
            prim_v[f, pl.ds(rows + 2 * width, width), :] = plane
            prim_v[f, pl.ds(rows + 3 * width, width), :] = plane

    @pl.when(soon)
    def _():
        hear(2, 2 + ring_near)
        heed(2)
        send_halos()

    pl.when(late)(functools.partial(hear, 1, half_n))

    for item in loads[3:]:
        item.wait()

    def spread(base, step, totals):
        device, k = base + step // 4, step % 4
        both = quad_v[device, pl.ds(pl.multiple_of(k * 8, 8), 8), :]
        values = (
            jnp.where(lane_block == 0, both, pltpu.roll(both, BT, 1)),
            jnp.where(lane_block == 1, both, pltpu.roll(both, 128 - BT, 1)),
        )
        for slot, value in zip((k, k + 4), values):
            index = (ring_pos * QUAD + device) * 8 + slot
            live = slot < count_s[ring_pos * QUAD + device]
            code = jnp.where(live, owner_s[index] * 2 + block_s[index], -1)
            relative = code - 2 * quad_pos - lane_block
            totals = tuple(
                total + jnp.where(relative == 2 * QUAD * z, value, 0.0)
                for z, total in enumerate(totals)
            )
        return totals

    totals = tuple(jnp.zeros((8, 128), F32) for _ in range(ring_n))
    own = quad_pos // 2 * 2
    quad_copies[0].wait()
    totals = lax.fori_loop(0, 8, functools.partial(spread, own), totals)
    quad_copies[1].wait()
    quad_copies[2].wait()
    totals = lax.fori_loop(0, 8, functools.partial(spread, 2 - own), totals)
    for k in range(ring_n):
        out_v[k] = totals[k]

    def ring_copy(to, slot):
        return remote(
            out_v.at[to], in_v.at[ring_pos], ring_send.at[slot], ring_recv.at[slot],
            to * QUAD + quad_pos, gz,
        )

    same_copies = [ring_copy(same_ring(step), step) for step in range(1, half_n)]
    other_copies = [
        ring_copy(half_n - half_at + p, half_n + (p + half_n - ring_pos + half_at) % half_n)
        for p in range(half_n)
    ]

    def send_same():
        for copy in same_copies:
            copy.start()

    def send_other():
        heed(1)
        pl.when(ahead_far)(ahead.start)
        across.start()
        for copy in other_copies:
            copy.start()
        pl.when(back_far)(back.start)

    @pl.when(early)
    def _():
        hear(3, half_n - 1 + jnp.where(soon, 0, 2 + ring_near))
        heed(3)
        send_same()
        pl.when(later)(send_halos)
        hear(1, half_n)
        send_other()

    @pl.when(late)
    def _():
        send_other()
        hear(3, half_n - 1 + 2 + ring_near)
        heed(3)
        send_halos()
        send_same()

    def sweep(load_plane, faces, normal, emit):
        before, cell = load_plane(0), load_plane(1)
        after = load_plane(2)
        diff = [b - a for a, b in zip(before, cell)]
        diff_up = [b - a for a, b in zip(cell, after)]
        left = [c + half_slope(a, b) for a, b, c in zip(diff, diff_up, cell)]

        def face(k, carry):
            cell, diff, left, flux_low = carry
            after = load_plane(k + 3)
            diff_up = [b - a for a, b in zip(cell, after)]
            slope = [half_slope(a, b) for a, b in zip(diff, diff_up)]
            right = [c - s for c, s in zip(cell, slope)]
            flux = double_flux(left, right, normal)
            return after, diff_up, [c + s for c, s in zip(cell, slope)], flux

        carry = face(0, (after, diff_up, left, None))

        def body(k, carry):
            low = carry[3]
            carry = face(k, carry)
            emit(k - 1, [b - a for a, b in zip(low, carry[3])])
            return carry

        lax.fori_loop(1, faces, body, carry)

    @pl.when(not_first)
    def _():
        up.wait_recv()
        down.wait_send()

    @pl.when(not_last)
    def _():
        up.wait_send()
        down.wait_recv()

    for half in range(2):

        def axial_plane(k):
            at = pl.multiple_of(k * width + half * 8, 8)
            return [prim_v[f, pl.ds(at, 8), :] for f in range(8)]

        def axial_emit(k, change):
            at = pl.ds(pl.multiple_of(k * width + half * 8, 8), 8)
            for f in range(8):
                res_ref[f, at, :] = res_ref[f, at, :] - 0.5 * change[f]

        sweep(axial_plane, depth + 1, 2, axial_emit)

    back.wait_recv()

    def theta_plane(k):
        return [cross_v[f, pl.ds(pl.multiple_of(k * depth, depth), depth), :] for f in range(8)]

    def theta_emit(k, change):
        for f in range(8):
            at = pl.ds(k, depth, stride=width)
            res_ref[f, at, :] = res_ref[f, at, :] - turn * change[f]

    sweep(lambda k: theta_plane(k + 2), width - 1, 1, lambda k, change: theta_emit(k + 2, change))

    across.wait()
    cell = [turned_v[f : f + 1, :] for f in range(8)]
    left = [
        cell[f]
        + half_slope(cell[f] - edge_in[f : f + 1, :], turned_v[8 + f : 9 + f, :])
        for f in range(8)
    ]
    face_one = jnp.concatenate(
        double_flux(left, [turned_v[16 + f : 17 + f, :] for f in range(8)], 0), axis=0
    )
    packed_v[...] = jnp.zeros_like(packed_v)
    packed_v[pl.ds(0, 8, stride=4), :] = -face_one
    packed_v[pl.ds(1, 8, stride=4), :] = face_one * (1.0 / 3.0)
    for z in range(depth):
        shift = (128 - z * width) % 128
        inner = 0.5 * face_one
        inner_ref[pl.ds(z, 8, stride=depth), :] = (
            pltpu.roll(inner, shift, 1) if shift else inner
        )[:, :width]

    for copy in same_copies + other_copies:
        copy.wait()
    registers = out_v[ring_pos]
    for step in range(1, ring_n):
        registers = registers + in_v[(ring_pos + step) % ring_n]
    mismatch = registers - coarse
    for z in range(depth):
        shift = (128 - z * width) % 128
        at = pl.ds(z, 8, stride=depth)
        mis_ref[at, :] = (pltpu.roll(mismatch, shift, 1) if shift else mismatch)[:, :width]
    face = (BR * level).astype(F32)
    added = mismatch * (face / (face + 0.5))
    for place in (BR, 2 * BR, 3 * BR):
        packed_v[pl.ds(place, 8, stride=4), :] = added
    corr_v[...] = packed_v[...].T

    ahead.wait_recv()
    sweep(theta_plane, 3, 1, theta_emit)

    ahead.wait_send()
    back.wait_send()

    hits = [(lane < 2) | (lane == BR * depth_of[half]) for half in range(2)]

    def correct(z, _):
        for half in range(2):
            at = pl.ds(pl.multiple_of(z * width + half * 8, 8), 8)
            corr = corr_v[at, :]
            for f in range(8):
                moved = pltpu.roll(corr, 128 - 4 * f, 1) if f else corr
                res_ref[f, at, :] = res_ref[f, at, :] + jnp.where(hits[half], moved, 0.0)
        return 0

    lax.fori_loop(0, depth, correct, 0, unroll=True)


def copy_out(*refs):
    count = len(refs) // 2
    copies = [
        pltpu.make_async_copy(refs[i], refs[count + i], refs[-1].at[i]) for i in range(count)
    ]
    for copy in copies:
        copy.start()
    for copy in copies:
        copy.wait()


def body(mesh_shape, fluid_state, levels, fine_rim, slot_owner, slot_block, slot_count):
    fields, depth, width, radial = fluid_state.shape
    theta_n, gz_n = mesh_shape
    rows = depth * width
    ring_n = theta_n // QUAD
    slots = fine_rim.shape[0]
    sizes = (theta_n, gz_n, depth, width, 2.0 * math.pi / (width * theta_n))
    hbm = pl.BlockSpec(memory_space=pltpu.MemorySpace.HBM)
    vmem = pl.BlockSpec(memory_space=pltpu.MemorySpace.VMEM)
    res, mis, inner = pl.pallas_call(
        functools.partial(kernel, sizes),
        out_shape=(
            jax.ShapeDtypeStruct((fields, rows, radial), F32),
            jax.ShapeDtypeStruct((fields * depth, width), F32),
            jax.ShapeDtypeStruct((fields * depth, width), F32),
        ),
        in_specs=[hbm] * 6,
        out_specs=(vmem, vmem, vmem),
        scratch_shapes=[
            pltpu.VMEM((fields, rows, radial), F32),
            pltpu.VMEM((slots * 2 * fields, 128), F32),
            pltpu.VMEM((fields, rows + 4 * width, radial), F32),
            pltpu.VMEM((fields, rows + 4 * depth, radial), F32),
            pltpu.VMEM((8, 128), F32),
            pltpu.VMEM((8, 128), F32),
            pltpu.VMEM((rows, 128), F32),
            pltpu.VMEM((128, rows), F32),
            pltpu.VMEM((rows, 128), F32),
            pltpu.VMEM((QUAD, slots * fields // 2, 128), F32),
            pltpu.VMEM((ring_n, 8, 128), F32),
            pltpu.VMEM((ring_n, 8, 128), F32),
            pltpu.SMEM((2, 4), jnp.int32),
            pltpu.SMEM(slot_owner.shape, jnp.int32),
            pltpu.SMEM(slot_block.shape, jnp.int32),
            pltpu.SMEM(slot_count.shape, jnp.int32),
            pltpu.SemaphoreType.DMA((6,)),
            pltpu.SemaphoreType.DMA((QUAD,)),
            pltpu.SemaphoreType.DMA((QUAD,)),
            pltpu.SemaphoreType.DMA((ring_n,)),
            pltpu.SemaphoreType.DMA((ring_n,)),
            pltpu.SemaphoreType.DMA((5,)),
            pltpu.SemaphoreType.DMA((5,)),
            pltpu.SemaphoreType.REGULAR((4,)),
        ],
        compiler_params=pltpu.CompilerParams(
            collective_id=0, has_side_effects=True, vmem_limit_bytes=32 * 1024 * 1024
        ),
    )(
        *(
            pltpu.with_memory_space_constraint(v, pltpu.MemorySpace.HBM)
            for v in (
                fluid_state.reshape(fields, rows, radial),
                fine_rim.reshape(slots * 2 * fields, 128),
                levels.T,
                slot_owner,
                slot_block,
                slot_count,
            )
        )
    )
    outs = (res, mis, inner)
    res, mis, inner = pl.pallas_call(
        copy_out,
        out_shape=tuple(jax.ShapeDtypeStruct(v.shape, F32) for v in outs),
        in_specs=[vmem] * 3,
        out_specs=(hbm,) * 3,
        scratch_shapes=[pltpu.SemaphoreType.DMA((3,))],
        compiler_params=pltpu.CompilerParams(vmem_limit_bytes=2 * 1024 * 1024),
    )(*outs)
    return (
        res.reshape(fields, depth, width, radial),
        mis.reshape(fields, depth, width),
        inner.reshape(fields, depth, width),
    )


def solution(mesh):
    return jax.shard_map(
        functools.partial(body, (mesh.shape["theta"], mesh.shape["gz"])),
        mesh=mesh,
        in_specs=(
            P(None, "gz", "theta", None),
            P(None, "theta"),
            P("theta", None, None, "gz"),
            P(),
            P(),
            P(),
        ),
        out_specs=(P(None, "gz", "theta", None), P(None, "gz", "theta"), P(None, "gz", "theta")),
        check_vma=False,
    )
```

```python
import functools
import math

import jax
import jax.numpy as jnp
from jax import lax
from jax.experimental import pallas as pl
from jax.experimental.pallas import tpu as pltpu
from jax.sharding import PartitionSpec as P

BT = 8
BR = 32
GAMMA = 5.0 / 3.0
QUAD = 4
F32 = jnp.float32
MESH = pl.DeviceIdType.MESH


def primitive(cons):
    rho, mr, mt, mz, energy, br, bt, bz = cons
    inv = 1.0 / rho
    vr, vt, vz = mr * inv, mt * inv, mz * inv
    kinetic = mr * vr + mt * vt + mz * vz
    magnetic = br * br + bt * bt + bz * bz
    pressure = (GAMMA - 1.0) * (energy - 0.5 * (kinetic + magnetic))
    return [rho, vr, vt, vz, pressure, br, bt, bz]


def side_state(state, normal):
    rho, pressure = state[0], state[4]
    vel, field = state[1:4], state[5:8]
    mom = [rho * v for v in vel]
    vel_n, field_n = vel[normal], field[normal]
    field_sq = field[0] * field[0] + field[1] * field[1] + field[2] * field[2]
    half_sq = 0.5 * field_sq
    kinetic = 0.5 * (mom[0] * vel[0] + mom[1] * vel[1] + mom[2] * vel[2])
    vel_dot = vel[0] * field[0] + vel[1] * field[1] + vel[2] * field[2]
    total_p = pressure + half_sq
    energy = pressure * (1.0 / (GAMMA - 1.0)) + kinetic + half_sq
    flux = [mom[normal]]
    for comp in range(3):
        term = mom[comp] * vel_n - field[comp] * field_n
        flux.append(term + total_p if comp == normal else term)
    flux.append((energy + total_p) * vel_n - field_n * vel_dot)
    for comp in range(3):
        flux.append(None if comp == normal else vel_n * field[comp] - field_n * vel[comp])
    fast = GAMMA * pressure + field_sq
    signal = jnp.abs(vel_n) + fast * lax.rsqrt(fast * rho)
    return [rho] + mom + [energy] + list(field), flux, signal


def double_flux(left, right, normal):
    cons_l, flux_l, signal_l = side_state(left, normal)
    cons_r, flux_r, signal_r = side_state(right, normal)
    top = jnp.maximum(signal_l, signal_r)
    out = []
    for ul, ur, fl, fr in zip(cons_l, cons_r, flux_l, flux_r):
        if fl is None:
            out.append(top * (ul - ur))
        else:
            out.append((fl + fr) - top * (ur - ul))
    return out


def half_slope(lower, upper):
    low, high = jnp.minimum(lower, upper), jnp.maximum(lower, upper)
    return 0.5 * (jnp.maximum(low, 0.0) + jnp.minimum(high, 0.0))


def kernel(
    sizes,
    x_hbm, fine_hbm, levels_hbm, owner_hbm, block_hbm, count_hbm,
    res_ref, mis_ref, inner_ref,
    x_v, fine_v, prim_v, cross_v, edge_v, edge_in, packed_v, turned_v, corr_v,
    quad_v, out_v, in_v,
    levels_s, owner_s, block_s, count_s,
    load_sem, quad_send, quad_recv, ring_send, ring_recv, halo_send, halo_recv, news_sem,
):
    theta_n, gz_n, depth, width, dtheta = sizes
    rows = depth * width
    ring_n = theta_n // QUAD
    theta = lax.axis_index("theta")
    gz = lax.axis_index("gz")
    ring_pos, quad_pos = theta // QUAD, theta % QUAD

    def load(src, dst, sem):
        return pltpu.make_async_copy(src, dst, load_sem.at[sem])

    loads = [
        load(fine_hbm, fine_v, 0),
        load(x_hbm, x_v, 1),
        load(levels_hbm, levels_s, 2),
        load(owner_hbm, owner_s, 3),
        load(block_hbm, block_s, 4),
        load(count_hbm, count_s, 5),
    ]
    for item in loads:
        item.start()

    barrier = pltpu.get_barrier_semaphore()
    half_n = ring_n // 2
    early = ring_pos < half_n
    late = jnp.logical_not(early)
    soon = ring_pos < half_n // 2
    later = jnp.logical_not(soon)
    half_at = ring_pos // half_n * half_n
    core_zero = quad_pos % 2 == 0
    not_start, not_end = ring_pos > half_at, ring_pos < half_at + half_n - 1
    ring_near = not_start.astype(jnp.int32) + not_end.astype(jnp.int32)

    def signal(sem, t, g):
        pl.semaphore_signal(sem, inc=1, device_id={"theta": t, "gz": g}, device_id_type=MESH)

    def same_ring(step):
        return half_at + (ring_pos - half_at + step) % half_n

    def other_ring(step):
        return half_n - half_at + (ring_pos - half_at + step) % half_n

    def hear(role, count):
        @pl.when(quad_pos == role)
        def _():
            pl.semaphore_wait(barrier, count)
            for step in range(1, QUAD):
                signal(news_sem.at[role], ring_pos * QUAD + (role + step) % QUAD, gz)

    def heed(role):
        @pl.when(quad_pos != role)
        def _():
            pl.semaphore_wait(news_sem.at[role], 1)

    @pl.when(quad_pos != 0)
    def _():
        signal(barrier, ring_pos * QUAD, gz)

    @pl.when(later & (quad_pos != 2))
    def _():
        signal(barrier, ring_pos * QUAD + 2, gz)

    lane = lax.broadcasted_iota(jnp.int32, (8, 128), 1)
    lane_block = (lane % width) // BT

    loads[0].wait()
    sides = [
        [fine_v[pl.ds(side * 8 + var, 8, stride=16), :] for var in range(8)] for side in (0, 1)
    ]
    fine_flux = jnp.concatenate(double_flux(sides[0], sides[1], 0), axis=0)
    src = lax.broadcasted_iota(jnp.int32, (128, 128), 0)
    dst = lax.broadcasted_iota(jnp.int32, (128, 128), 1)
    pairing = jnp.where(
        (src // width == dst // width) & ((src % width) // 2 == dst % BT), 0.125, 0.0
    ).astype(F32)
    partial = jnp.dot(
        fine_flux, pairing, precision=lax.Precision.HIGHEST, preferred_element_type=F32
    )
    for var in range(8):
        rows_var = partial[var * 8 : var * 8 + 8]
        pair = jnp.where(lane_block == 0, rows_var, pltpu.roll(rows_var, 4, 0))
        quad_v[quad_pos, pl.ds(var, 4, stride=8), :] = pair[0:4]

    def remote(src, dst, send, recv, t, g):
        return pltpu.make_async_remote_copy(
            src_ref=src, dst_ref=dst, send_sem=send, recv_sem=recv,
            device_id={"theta": t, "gz": g}, device_id_type=MESH,
        )

    partners = [quad_pos + 1 - 2 * (quad_pos % 2), (quad_pos + 2) % QUAD, QUAD - 1 - quad_pos]
    quad_copies = [
        remote(
            quad_v.at[quad_pos], quad_v.at[quad_pos], quad_send.at[i], quad_recv.at[i],
            ring_pos * QUAD + partner, gz,
        )
        for i, partner in enumerate(partners)
    ]
    gz_next, gz_back = (gz + 1) % gz_n, (gz + gz_n - 1) % gz_n

    def greet_near():
        signal(barrier, theta, gz_next)
        signal(barrier, theta, gz_back)
        for there, r in ((not_start, ring_pos - 1), (not_end, ring_pos + 1)):
            role = jnp.where((r >= 0) & (r < half_n // 2), 2, 3)
            pl.when(there)(functools.partial(signal, barrier, r * QUAD + role, gz))

    def start_quad():
        pl.when(soon)(functools.partial(hear, 0, QUAD - 1))

        @pl.when(later & core_zero)
        def _():
            wraps = (ring_pos == ring_n - 1) & (quad_pos == 2)
            pl.semaphore_wait(barrier, QUAD - 1 + wraps.astype(jnp.int32))
            signal(news_sem.at[0], theta + 1, gz)

        @pl.when((soon & (quad_pos != 0)) | (later & jnp.logical_not(core_zero)))
        def _():
            pl.semaphore_wait(news_sem.at[0], 1)

        @pl.when((ring_pos == 0) & (quad_pos == 2))
        def _():
            signal(barrier, (ring_n - 1) * QUAD + 2, gz)

        for i in (1, 2, 0):
            quad_copies[i].start()

        @pl.when(quad_pos == 1)
        def _():
            for step in range(half_n):
                signal(barrier, other_ring(step) * QUAD + 1, gz)

        pl.when(soon & (quad_pos == 2))(greet_near)

        @pl.when(quad_pos == 3)
        def _():
            pl.when(later)(greet_near)
            for step in range(1, half_n):
                signal(barrier, same_ring(step) * QUAD + 3, gz)

    upper = quad_pos >= QUAD // 2
    pl.when(upper)(start_quad)

    loads[1].wait()

    def to_primitive(z, _):
        at = pl.multiple_of(z * width, width)
        for half in range(2):
            prims = primitive([x_v[f, pl.ds(at + half * 8, 8), :] for f in range(8)])
            for f, value in enumerate(prims):
                prim_v[f, pl.ds(at + 2 * width + half * 8, 8), :] = value
                cross_v[f, pl.ds((2 + half * 8) * depth + z, 8, stride=depth), :] = value
        return 0

    lax.fori_loop(0, depth, to_primitive, 0)

    ahead = remote(
        cross_v.at[:, pl.ds(rows, 2 * depth)], cross_v.at[:, pl.ds(0, 2 * depth)],
        halo_send.at[3], halo_recv.at[3], (theta + 1) % theta_n, gz,
    )
    at_end = theta == theta_n - 1
    pl.when(at_end)(ahead.start)

    radius = lane.astype(F32) + 0.5
    inv_radius = 1.0 / radius
    inward = jnp.where(lane == 1, 0.0, 0.5 * (radius - 0.5) * inv_radius)
    outward = jnp.where(lane == 0, 0.0, 0.5 * (radius + 0.5) * inv_radius)
    turn = inv_radius * (0.5 / dtheta)
    last = lane == 127
    spot = jnp.where(lane >= BR, lane % BR, -1)

    def radial(z, _):
        for half in range(2):
            at = pl.multiple_of(z * width + half * 8, 8)
            left, right = [], []
            cell = [prim_v[f, pl.ds(at + 2 * width, 8), :] for f in range(8)]
            packed = jnp.zeros((8, 128), F32)
            for f in range(8):
                mid = cell[f]
                lower = mid - pltpu.roll(mid, 1, 1)
                upper = jnp.where(last, 0.0, pltpu.roll(lower, 127, 1))
                slope = half_slope(lower, upper)
                left.append(mid + slope)
                right.append(jnp.where(last, mid, pltpu.roll(mid - slope, 127, 1)))
                packed = jnp.where(lane == f, pltpu.roll(mid, f, 1) if f else mid, packed)
                packed = jnp.where(lane == f + 8, pltpu.roll(upper, f + 8, 1), packed)
                packed = jnp.where(lane == f + 16, pltpu.roll(right[f], f + 16, 1), packed)
            flux = double_flux(left, right, 0)
            rho, vr, vt, _, pressure, br, bt, bz = cell
            out = [inward * pltpu.roll(v, 1, 1) - outward * v for v in flux]
            field_sq = br * br + bt * bt + bz * bz
            out[1] = out[1] + inv_radius * (rho * vt * vt + pressure + 0.5 * field_sq - bt * bt)
            out[2] = out[2] - inv_radius * (rho * vr * vt - br * bt)
            out[6] = out[6] + inv_radius * (vr * bt - vt * br)
            for f in range(8):
                res_ref[f, pl.ds(at, 8), :] = out[f]
                packed = jnp.where(spot == f, pltpu.roll(flux[f], f + 1, 1), packed)
            packed_v[pl.ds(at, 8), :] = packed
        return 0

    lax.fori_loop(0, depth // 2, radial, 0)
    pl.when(jnp.logical_not(upper))(start_quad)
    lax.fori_loop(depth // 2, depth, radial, 0)
    turned_v[...] = packed_v[...].T
    row = lax.broadcasted_iota(jnp.int32, (8, 128), 0)
    flip = (row == 1) | (row == 2) | (row == 5) | (row == 6)
    edge_v[...] = jnp.where(flip, -turned_v[0:8, :], turned_v[0:8, :])

    loads[2].wait()
    depth_of = [levels_s[b, 0] + levels_s[b, 1] + levels_s[b, 2] + levels_s[b, 3] for b in range(2)]
    level = jnp.where(lane_block == 0, depth_of[0], depth_of[1])
    coarse = 0.5 * jnp.where(
        level == 1,
        turned_v[BR : BR + 8, :],
        jnp.where(level == 2, turned_v[2 * BR : 2 * BR + 8, :], turned_v[3 * BR : 3 * BR + 8, :]),
    )

    across = remote(
        edge_v, edge_in, halo_send.at[0], halo_recv.at[0], (theta + theta_n // 2) % theta_n, gz
    )
    two_z, two_t = 2 * width, 2 * depth
    up = remote(
        prim_v.at[:, pl.ds(rows, two_z)], prim_v.at[:, pl.ds(0, two_z)],
        halo_send.at[1], halo_recv.at[1], theta, (gz + 1) % gz_n,
    )
    down = remote(
        prim_v.at[:, pl.ds(two_z, two_z)], prim_v.at[:, pl.ds(rows + two_z, two_z)],
        halo_send.at[2], halo_recv.at[2], theta, (gz + gz_n - 1) % gz_n,
    )
    not_last, not_first = gz < gz_n - 1, gz > 0
    back = remote(
        cross_v.at[:, pl.ds(two_t, two_t)], cross_v.at[:, pl.ds(rows + two_t, two_t)],
        halo_send.at[4], halo_recv.at[4], (theta + theta_n - 1) % theta_n, gz,
    )

    ahead_far = (theta + 1) % (theta_n // 2) == 0
    back_far = theta % (theta_n // 2) == 0

    def send_halos():
        pl.when(jnp.logical_not(ahead_far))(ahead.start)
        pl.when(jnp.logical_not(back_far))(back.start)
        pl.when(not_last)(up.start)
        pl.when(not_first)(down.start)

    @pl.when(gz == 0)
    def _():
        for f in range(8):
            plane = prim_v[f, pl.ds(two_z, width), :]
            prim_v[f, pl.ds(0, width), :] = plane
            prim_v[f, pl.ds(width, width), :] = plane

    @pl.when(gz == gz_n - 1)
    def _():
        for f in range(8):
            plane = prim_v[f, pl.ds(rows + width, width), :]
            prim_v[f, pl.ds(rows + 2 * width, width), :] = plane
            prim_v[f, pl.ds(rows + 3 * width, width), :] = plane

    @pl.when(soon)
    def _():
        hear(2, 2 + ring_near)
        heed(2)
        send_halos()

    pl.when(late)(functools.partial(hear, 1, half_n))

    for item in loads[3:]:
        item.wait()

    def spread(base, step, totals):
        device, k = base + step // 4, step % 4
        both = quad_v[device, pl.ds(pl.multiple_of(k * 8, 8), 8), :]
        values = (
            jnp.where(lane_block == 0, both, pltpu.roll(both, BT, 1)),
            jnp.where(lane_block == 1, both, pltpu.roll(both, 128 - BT, 1)),
        )
        for slot, value in zip((k, k + 4), values):
            index = (ring_pos * QUAD + device) * 8 + slot
            live = slot < count_s[ring_pos * QUAD + device]
            code = jnp.where(live, owner_s[index] * 2 + block_s[index], -1)
            relative = code - 2 * quad_pos - lane_block
            totals = tuple(
                total + jnp.where(relative == 2 * QUAD * z, value, 0.0)
                for z, total in enumerate(totals)
            )
        return totals

    totals = tuple(jnp.zeros((8, 128), F32) for _ in range(ring_n))
    own = quad_pos // 2 * 2
    quad_copies[0].wait()
    totals = lax.fori_loop(0, 8, functools.partial(spread, own), totals)
    quad_copies[1].wait()
    quad_copies[2].wait()
    totals = lax.fori_loop(0, 8, functools.partial(spread, 2 - own), totals)
    for k in range(ring_n):
        out_v[k] = totals[k]

    def ring_copy(to, slot):
        return remote(
            out_v.at[to], in_v.at[ring_pos], ring_send.at[slot], ring_recv.at[slot],
            to * QUAD + quad_pos, gz,
        )

    same_copies = [ring_copy(same_ring(step), step) for step in range(1, half_n)]
    other_copies = [
        ring_copy(half_n - half_at + p, half_n + (p + half_n - ring_pos + half_at) % half_n)
        for p in range(half_n)
    ]

    def send_same():
        for copy in same_copies:
            copy.start()

    def send_other():
        heed(1)
        pl.when(ahead_far & jnp.logical_not(at_end))(ahead.start)
        across.start()
        for copy in other_copies:
            copy.start()
        pl.when(back_far)(back.start)

    @pl.when(early)
    def _():
        hear(3, half_n - 1 + jnp.where(soon, 0, 2 + ring_near))
        heed(3)
        send_same()
        pl.when(later)(send_halos)
        hear(1, half_n)
        send_other()

    @pl.when(late)
    def _():
        send_other()
        hear(3, half_n - 1 + 2 + ring_near)
        heed(3)
        send_halos()
        send_same()

    def sweep(load_plane, faces, normal, emit):
        before, cell = load_plane(0), load_plane(1)
        after = load_plane(2)
        diff = [b - a for a, b in zip(before, cell)]
        diff_up = [b - a for a, b in zip(cell, after)]
        left = [c + half_slope(a, b) for a, b, c in zip(diff, diff_up, cell)]

        def face(k, carry):
            cell, diff, left, flux_low = carry
            after = load_plane(k + 3)
            diff_up = [b - a for a, b in zip(cell, after)]
            slope = [half_slope(a, b) for a, b in zip(diff, diff_up)]
            right = [c - s for c, s in zip(cell, slope)]
            flux = double_flux(left, right, normal)
            return after, diff_up, [c + s for c, s in zip(cell, slope)], flux

        carry = face(0, (after, diff_up, left, None))

        def body(k, carry):
            low = carry[3]
            carry = face(k, carry)
            emit(k - 1, [b - a for a, b in zip(low, carry[3])])
            return carry

        lax.fori_loop(1, faces, body, carry)

    @pl.when(not_first)
    def _():
        up.wait_recv()
        down.wait_send()

    @pl.when(not_last)
    def _():
        up.wait_send()
        down.wait_recv()

    for half in range(2):

        def axial_plane(k):
            at = pl.multiple_of(k * width + half * 8, 8)
            return [prim_v[f, pl.ds(at, 8), :] for f in range(8)]

        def axial_emit(k, change):
            at = pl.ds(pl.multiple_of(k * width + half * 8, 8), 8)
            for f in range(8):
                res_ref[f, at, :] = res_ref[f, at, :] - 0.5 * change[f]

        sweep(axial_plane, depth + 1, 2, axial_emit)

    back.wait_recv()

    def theta_plane(k):
        return [cross_v[f, pl.ds(pl.multiple_of(k * depth, depth), depth), :] for f in range(8)]

    def theta_emit(k, change):
        for f in range(8):
            at = pl.ds(k, depth, stride=width)
            res_ref[f, at, :] = res_ref[f, at, :] - turn * change[f]

    sweep(lambda k: theta_plane(k + 2), width - 1, 1, lambda k, change: theta_emit(k + 2, change))

    across.wait()
    cell = [turned_v[f : f + 1, :] for f in range(8)]
    left = [
        cell[f]
        + half_slope(cell[f] - edge_in[f : f + 1, :], turned_v[8 + f : 9 + f, :])
        for f in range(8)
    ]
    face_one = jnp.concatenate(
        double_flux(left, [turned_v[16 + f : 17 + f, :] for f in range(8)], 0), axis=0
    )
    packed_v[...] = jnp.zeros_like(packed_v)
    packed_v[pl.ds(0, 8, stride=4), :] = -face_one
    packed_v[pl.ds(1, 8, stride=4), :] = face_one * (1.0 / 3.0)
    for z in range(depth):
        shift = (128 - z * width) % 128
        inner = 0.5 * face_one
        inner_ref[pl.ds(z, 8, stride=depth), :] = (
            pltpu.roll(inner, shift, 1) if shift else inner
        )[:, :width]

    for copy in same_copies + other_copies:
        copy.wait()
    registers = out_v[ring_pos]
    for step in range(1, ring_n):
        registers = registers + in_v[(ring_pos + step) % ring_n]
    mismatch = registers - coarse
    for z in range(depth):
        shift = (128 - z * width) % 128
        at = pl.ds(z, 8, stride=depth)
        mis_ref[at, :] = (pltpu.roll(mismatch, shift, 1) if shift else mismatch)[:, :width]
    face = (BR * level).astype(F32)
    added = mismatch * (face / (face + 0.5))
    for place in (BR, 2 * BR, 3 * BR):
        packed_v[pl.ds(place, 8, stride=4), :] = added
    corr_v[...] = packed_v[...].T

    ahead.wait_recv()
    sweep(theta_plane, 3, 1, theta_emit)

    ahead.wait_send()
    back.wait_send()

    hits = [(lane < 2) | (lane == BR * depth_of[half]) for half in range(2)]

    def correct(z, _):
        for half in range(2):
            at = pl.ds(pl.multiple_of(z * width + half * 8, 8), 8)
            corr = corr_v[at, :]
            for f in range(8):
                moved = pltpu.roll(corr, 128 - 4 * f, 1) if f else corr
                res_ref[f, at, :] = res_ref[f, at, :] + jnp.where(hits[half], moved, 0.0)
        return 0

    lax.fori_loop(0, depth, correct, 0, unroll=True)


def copy_out(*refs):
    count = len(refs) // 2
    copies = [
        pltpu.make_async_copy(refs[i], refs[count + i], refs[-1].at[i]) for i in range(count)
    ]
    for copy in copies:
        copy.start()
    for copy in copies:
        copy.wait()


def body(mesh_shape, fluid_state, levels, fine_rim, slot_owner, slot_block, slot_count):
    fields, depth, width, radial = fluid_state.shape
    theta_n, gz_n = mesh_shape
    rows = depth * width
    ring_n = theta_n // QUAD
    slots = fine_rim.shape[0]
    sizes = (theta_n, gz_n, depth, width, 2.0 * math.pi / (width * theta_n))
    hbm = pl.BlockSpec(memory_space=pltpu.MemorySpace.HBM)
    vmem = pl.BlockSpec(memory_space=pltpu.MemorySpace.VMEM)
    res, mis, inner = pl.pallas_call(
        functools.partial(kernel, sizes),
        out_shape=(
            jax.ShapeDtypeStruct((fields, rows, radial), F32),
            jax.ShapeDtypeStruct((fields * depth, width), F32),
            jax.ShapeDtypeStruct((fields * depth, width), F32),
        ),
        in_specs=[hbm] * 6,
        out_specs=(vmem, vmem, vmem),
        scratch_shapes=[
            pltpu.VMEM((fields, rows, radial), F32),
            pltpu.VMEM((slots * 2 * fields, 128), F32),
            pltpu.VMEM((fields, rows + 4 * width, radial), F32),
            pltpu.VMEM((fields, rows + 4 * depth, radial), F32),
            pltpu.VMEM((8, 128), F32),
            pltpu.VMEM((8, 128), F32),
            pltpu.VMEM((rows, 128), F32),
            pltpu.VMEM((128, rows), F32),
            pltpu.VMEM((rows, 128), F32),
            pltpu.VMEM((QUAD, slots * fields // 2, 128), F32),
            pltpu.VMEM((ring_n, 8, 128), F32),
            pltpu.VMEM((ring_n, 8, 128), F32),
            pltpu.SMEM((2, 4), jnp.int32),
            pltpu.SMEM(slot_owner.shape, jnp.int32),
            pltpu.SMEM(slot_block.shape, jnp.int32),
            pltpu.SMEM(slot_count.shape, jnp.int32),
            pltpu.SemaphoreType.DMA((6,)),
            pltpu.SemaphoreType.DMA((QUAD,)),
            pltpu.SemaphoreType.DMA((QUAD,)),
            pltpu.SemaphoreType.DMA((ring_n,)),
            pltpu.SemaphoreType.DMA((ring_n,)),
            pltpu.SemaphoreType.DMA((5,)),
            pltpu.SemaphoreType.DMA((5,)),
            pltpu.SemaphoreType.REGULAR((4,)),
        ],
        compiler_params=pltpu.CompilerParams(
            collective_id=0, has_side_effects=True, vmem_limit_bytes=32 * 1024 * 1024
        ),
    )(
        *(
            pltpu.with_memory_space_constraint(v, pltpu.MemorySpace.HBM)
            for v in (
                fluid_state.reshape(fields, rows, radial),
                fine_rim.reshape(slots * 2 * fields, 128),
                levels.T,
                slot_owner,
                slot_block,
                slot_count,
            )
        )
    )
    outs = (res, mis, inner)
    res, mis, inner = pl.pallas_call(
        copy_out,
        out_shape=tuple(jax.ShapeDtypeStruct(v.shape, F32) for v in outs),
        in_specs=[vmem] * 3,
        out_specs=(hbm,) * 3,
        scratch_shapes=[pltpu.SemaphoreType.DMA((3,))],
        compiler_params=pltpu.CompilerParams(vmem_limit_bytes=2 * 1024 * 1024),
    )(*outs)
    return (
        res.reshape(fields, depth, width, radial),
        mis.reshape(fields, depth, width),
        inner.reshape(fields, depth, width),
    )


def solution(mesh):
    return jax.shard_map(
        functools.partial(body, (mesh.shape["theta"], mesh.shape["gz"])),
        mesh=mesh,
        in_specs=(
            P(None, "gz", "theta", None),
            P(None, "theta"),
            P("theta", None, None, "gz"),
            P(),
            P(),
            P(),
        ),
        out_specs=(P(None, "gz", "theta", None), P(None, "gz", "theta"), P(None, "gz", "theta")),
        check_vma=False,
    )
```
